32 devices in a mesh: section: 4 (over z), seq: 4 (over y, x), tp: 2 (over core).
Axes of the slice: x: 2, y: 2, z: 4, core: 2. Of those that a mesh axis runs over, the one named last changes fastest.
Arguments:
- queries: bfloat16 [4, 512, 8192], P('section', 'seq', 'tp'), may hold values from -64 to 64
- picture_key_matrix: bfloat16 [4, 32, 1024], P('section', ('seq', 'tp')), may hold values from -8 to 8
- picture_value_matrix: bfloat16 [4, 32, 1024], P('section', ('seq', 'tp')), may hold values from -6 to 6
- cotangent: bfloat16 [4, 512, 8192], P('section', 'seq', 'tp'), may hold values from -6 to 6
- pattern: int32 [4, 4, 4], P('section', 'seq'), may hold values from 0 to 1, as said below
- tile_owner: int32 [4, 4], P('section'), may hold values from 0 to 3, each once within a row
Outputs:
- attended: bfloat16 [4, 512, 8192], P('section', 'seq', 'tp')
- grad_queries: bfloat16 [4, 512, 8192], P('section', 'seq', 'tp')
- grad_keys: bfloat16 [4, 32, 1024], P('section', 'seq', 'tp')
- grad_values: bfloat16 [4, 32, 1024], P('section', 'seq', 'tp')
The draws below stay inside these ranges and needn't reach their ends.
Inputs may be any that keep to these rules, and one draw needn't show every extreme that they name: `pattern`: every text block attends to at least one and at most four tiles. `tile_owner`: each slot's row is a permutation: every row block holds exactly one tile.
All inputs are finite; a program needn't handle non-finite values.
Results may differ from the reference program's by a relative error of at most 0.0092.
Values may be sent and summed in bfloat16 or wider, within the bound.
A program may use at most 64 MiB of HBM per device.

```python
import jax
import jax.numpy as jnp
from jax import lax

QUERY_HEADS = 64
KEY_VALUE_HEADS = 8
HEAD_SIZE = 128
TILE_TOK = 8
BLOCK = 128
TEXT = 512
TILES = 4
IMAGE_TOKENS = 32
TEXT_BLOCKS = 4
N_SECTION = 4


def draw_pair(key):
    base = jax.random.fold_in(key, 31)
    key_query, random_key_split = jax.random.split(base, 2)
    picture_key_matrix = jax.random.normal(random_key_split, (N_SECTION, IMAGE_TOKENS, KEY_VALUE_HEADS * HEAD_SIZE), jnp.float32)
    queries = jax.random.normal(key_query, (N_SECTION, TEXT, QUERY_HEADS * HEAD_SIZE), jnp.float32)
    return (queries, picture_key_matrix)


def draw_queries(key, part):
    return draw_pair(key)[0].astype(jnp.bfloat16)


def draw_picture_key_matrix(key, part):
    return draw_pair(key)[1].astype(jnp.bfloat16)


def draw_pattern(key, part):
    base = jax.random.fold_in(key, 5)
    key_count, key_score = jax.random.split(base, 2)
    most = min(4, TILES)
    counts = jax.random.randint(key_count, (N_SECTION, TEXT_BLOCKS, 1), 1, most + 1)
    scores = jax.random.randint(key_score, (N_SECTION, TEXT_BLOCKS, TILES), 0, 1 << 20) * TILES + jnp.arange(TILES, dtype=jnp.int32)[None, None, :]
    ranks = jnp.argsort(jnp.argsort(scores, axis=-1), axis=-1)
    return (ranks < counts).astype(jnp.int32)


def block_levels(stream_key, dims, pieces, least, top_value):
    def one(position, shards_of):
        draws = jax.random.uniform(jax.random.fold_in(jax.random.fold_in(stream_key, 6), position), (shards_of,), jnp.float32, least / len(pieces), top_value / len(pieces))
        return jnp.repeat(jnp.exp(draws), dims[position] // shards_of).reshape((-1,) + (1,) * (len(dims) - position - 1))

    level = one(*pieces[0])
    for cut in pieces[1:]:
        level = level * one(*cut)
    return level


def gaussian(stream_key, extent, spread, most, shards=(), kind=jnp.bfloat16):
    drawn = jax.random.normal(stream_key, extent, jnp.float32) * spread
    if len(shards) > 0:
        drawn = block_levels(stream_key, extent, shards, -0.22, 0.18) * drawn
    return jnp.clip(drawn, min=-most, max=most).astype(kind)


def setup_inputs(seed: int = 0) -> dict:
    seeds = jax.random.split(jax.random.key(seed), 7)
    return {
        "queries": draw_queries(jax.random.fold_in(seeds[6], 71), 0),
        "picture_key_matrix": draw_picture_key_matrix(jax.random.fold_in(seeds[6], 71), 0),
        "picture_value_matrix": gaussian(seeds[2], (N_SECTION, IMAGE_TOKENS, KEY_VALUE_HEADS * HEAD_SIZE), 1.0, 6.0, ((0, 4), (1, 8))),
        "cotangent": gaussian(seeds[3], (N_SECTION, TEXT, QUERY_HEADS * HEAD_SIZE), 1.0, 6.0, ((0, 4), (1, 4), (2, 2))),
        "pattern": draw_pattern(jax.random.fold_in(seeds[6], 71), 0),
        "tile_owner": jax.vmap(lambda own: jax.random.permutation(own, TILES))(jax.random.split(seeds[5], N_SECTION)).reshape((N_SECTION, TILES)).astype(jnp.int32),
    }


def token_mask(pattern_slot, owner_slot):
    hits = (owner_slot[:, None] == jnp.arange(TILES, dtype=jnp.int32)[None, :]).astype(jnp.float32)
    allowed = jnp.dot(pattern_slot.astype(jnp.float32), hits) > 0.5
    return jnp.repeat(jnp.repeat(allowed, BLOCK, axis=0), TILE_TOK, axis=1)


def attend_group(query_group, key_group, value_group, cot_group, mask):
    scale = HEAD_SIZE ** -0.5
    scores = jnp.einsum('thd,jd->htj', query_group, key_group) * scale
    scores = jnp.where(mask[None], scores, -jnp.inf)
    top = jnp.max(scores, axis=-1, keepdims=True)
    expo = jnp.exp(scores - top)
    probs = expo / jnp.sum(expo, axis=-1, keepdims=True)
    probs_low = lax.optimization_barrier(probs.astype(jnp.bfloat16)).astype(jnp.float32)
    output = jnp.einsum('htj,jd->thd', probs_low, value_group)
    out_low = lax.optimization_barrier(output.astype(jnp.bfloat16))
    delta = jnp.einsum('thd,thd->ht', cot_group, out_low.astype(jnp.float32))
    dprobs = jnp.einsum('thd,jd->htj', cot_group, value_group)
    dscores = probs * (dprobs - delta[:, :, None])
    ds_low = lax.optimization_barrier(dscores.astype(jnp.bfloat16)).astype(jnp.float32)
    grad_query = (jnp.einsum('htj,jd->thd', ds_low, key_group) * scale).astype(jnp.bfloat16)
    grad_key = jnp.einsum('htj,thd->jd', ds_low, query_group) * scale
    grad_value = jnp.einsum('htj,thd->jd', probs_low, cot_group)
    return out_low, grad_query, grad_key, grad_value


def one_slot(items):
    queries, picture_key_matrix, picture_value_matrix, rolled, pattern, tile_owner = items
    mask = token_mask(pattern, tile_owner)
    head_group = QUERY_HEADS // KEY_VALUE_HEADS
    outs, grad_qs, grad_ks, grad_vs = [], [], [], []
    for key_value_head in range(KEY_VALUE_HEADS):
        query_group = queries[:, key_value_head * head_group * HEAD_SIZE:(key_value_head + 1) * head_group * HEAD_SIZE].astype(jnp.float32).reshape(TEXT, head_group, HEAD_SIZE)
        cot_group = rolled[:, key_value_head * head_group * HEAD_SIZE:(key_value_head + 1) * head_group * HEAD_SIZE].astype(jnp.float32).reshape(TEXT, head_group, HEAD_SIZE)
        key_group = picture_key_matrix[:, key_value_head * HEAD_SIZE:(key_value_head + 1) * HEAD_SIZE].astype(jnp.float32)
        value_group = picture_value_matrix[:, key_value_head * HEAD_SIZE:(key_value_head + 1) * HEAD_SIZE].astype(jnp.float32)
        out_low, grad_query, grad_key, grad_value = attend_group(query_group, key_group, value_group, cot_group, mask)
        outs.append(out_low.reshape(TEXT, head_group * HEAD_SIZE))
        grad_qs.append(grad_query.reshape(TEXT, head_group * HEAD_SIZE))
        grad_ks.append(grad_key)
        grad_vs.append(grad_value)
    return (jnp.concatenate(outs, 1), jnp.concatenate(grad_qs, 1),
            jnp.concatenate(grad_ks, 1).astype(jnp.bfloat16), jnp.concatenate(grad_vs, 1).astype(jnp.bfloat16))


def reference(queries, picture_key_matrix, picture_value_matrix, cotangent, pattern, tile_owner):
    rolled = jnp.roll(cotangent, -1, axis=0)
    attended, grad_queries, grad_keys, grad_values = lax.map(one_slot, (queries, picture_key_matrix, picture_value_matrix, rolled, pattern, tile_owner))
    return attended, grad_queries, grad_keys, grad_values
```

```python
import functools

import jax
import jax.numpy as jnp
from jax import lax
from jax.experimental import pallas as pl
from jax.experimental.pallas import tpu as pltpu
from jax.sharding import PartitionSpec as P

QUERY_HEADS = 64
KEY_VALUE_HEADS = 8
HEAD_SIZE = 128
FAN = QUERY_HEADS // KEY_VALUE_HEADS
PACK = 4
CUTS = 4
MESH = pl.DeviceIdType.MESH
F32 = jnp.float32
BF16 = jnp.bfloat16


def nt(a, b):
    return lax.dot_general(a, b, (((1,), (1,)), ((), ())), preferred_element_type=F32)


def nn(a, b):
    return lax.dot_general(a, b, (((1,), (0,)), ((), ())), preferred_element_type=F32)


def tn(a, b):
    return lax.dot_general(a, b, (((0,), (0,)), ((), ())), preferred_element_type=F32)


def kernel(
    nsec, nseq, ntp,
    q_hbm, k_hbm, v_hbm, c_hbm, pat, own,
    att_vm, gq_vm, gk_out, gv_out,
    q_vm, c_vm, raw_vm,
    kv_st, kvg, asm, v_own, v_up,
    k_bd, v_bd,
    p_f32, p_send, p_recv, dp_send, dp_recv,
    dk_t, dk_r, dv_t, dv_r, rv_t, rv_r,
    load_sem, st_sem, own_sem,
    kv_ss, kv_rs, v_sem, raw_sem,
    p_ss, p_rs, dp_ss, dp_rs,
    dk_ss, dk_rs, dv_ss, dv_rs, rv_ss, rv_rs,
    ready_up, ready_down,
):
    scale = HEAD_SIZE ** (-0.5)
    D = HEAD_SIZE
    n = nseq * ntp
    text, cols = q_vm.shape
    part = k_hbm.shape[1]
    width = k_hbm.shape[2] // ntp
    rows = part * n
    groups = width // D
    share = rows // nseq
    lots = FAN // PACK
    lot = PACK * rows
    wide = PACK * D
    sec, seq, tp = lax.axis_index("section"), lax.axis_index("seq"), lax.axis_index("tp")
    me = seq * ntp + tp
    up, down = lax.rem(sec + 1, nsec), lax.rem(sec + nsec - 1, nsec)
    last = nsec - 1

    def dev(s, i):
        return {"section": s, "seq": lax.div(i, ntp), "tp": lax.rem(i, ntp)}

    def signal(sem, to):
        pl.semaphore_signal(sem, inc=1, device_id=to, device_id_type=MESH)

    def remote(src, dst, ss, rs, to):
        return pltpu.make_async_remote_copy(
            src_ref=src, dst_ref=dst, send_sem=ss, recv_sem=rs, device_id=to, device_id_type=MESH
        )

    barrier = pltpu.get_barrier_semaphore()
    for d in range(1, n):
        signal(barrier, dev(sec, lax.rem(me + n - d, n)))

    @pl.when(sec < last)
    def _():
        signal(barrier, dev(up, me))

    @pl.when(sec == 0)
    def _():
        signal(barrier, dev(down, me))

    stage = []
    for t in range(ntp):
        at = slice(t * width, (t + 1) * width)
        stage.append(pltpu.make_async_copy(k_hbm.at[0, :, at], kv_st.at[t, 0], st_sem.at[t, 0]))
        stage.append(pltpu.make_async_copy(v_hbm.at[0, :, at], kv_st.at[t, 1], st_sem.at[t, 1]))
    for c in stage:
        c.start()
    loads = [
        pltpu.make_async_copy(q_hbm.at[0], q_vm, load_sem.at[0]),
        pltpu.make_async_copy(c_hbm.at[0], c_vm, load_sem.at[1]),
    ]
    for c in loads:
        c.start()

    row_tile = lax.broadcasted_iota(jnp.int32, (rows, text), 0) // (rows // own.shape[1])
    blocks = pat.shape[1]
    lane_block = lax.broadcasted_iota(jnp.int32, (rows, text), 1) // (text // blocks)
    allowed = jnp.zeros((rows, text), jnp.bool_)
    for b in range(blocks):
        for t in range(own.shape[1]):
            owner = jnp.where(pat[0, b, t] > 0, own[0, t], -1)
            hit = row_tile == owner
            if blocks > 1:
                hit = hit & (lane_block == b)
            allowed = allowed | hit
    k_bd[...] = jnp.zeros_like(k_bd)
    v_bd[...] = jnp.zeros_like(v_bd)

    for c in stage:
        c.wait()
    mine = pltpu.make_async_copy(kv_st.at[tp], kvg.at[me], own_sem.at[0])
    mine.start()

    from_others = jnp.where(sec > 0, 1, 0) + jnp.where(sec == last, 1, 0)
    pl.semaphore_wait(barrier, n - 1 + from_others)

    @pl.when(sec > 0)
    def _():
        signal(ready_up, dev(down, me))

    @pl.when(sec == last)
    def _():
        signal(ready_down, dev(up, me))

    kv_copies = []
    for d in range(1, n):
        peer = lax.rem(me + n - d, n)
        c = remote(kv_st.at[lax.rem(peer, ntp)], kvg.at[me], kv_ss.at[d], kv_rs.at[d], dev(sec, peer))
        c.start()
        kv_copies.append(c)

    raw = remote(
        c_hbm.at[0, :, 0:wide], raw_vm, raw_sem.at[0], raw_sem.at[1], dev(down, me)
    )

    @pl.when(sec > 0)
    def _():
        raw.start()

    def assemble(which):
        for i in range(n):
            asm[which, part * i : part * (i + 1), :] = kvg[i, which].astype(F32)

    def heads(ref, g, a, b):
        j = (g * lots + a) * PACK + b
        return ref[:, j * D : (j + 1) * D]

    chunks = [(g, a) for g in range(groups) for a in range(lots)]
    RAW = chunks[0]

    mine.wait()
    for c in kv_copies:
        c.wait_recv()
    assemble(0)
    keys = [asm[0, :, g * D : (g + 1) * D].astype(BF16) for g in range(groups)]
    loads[0].wait()
    p_copies, dp_copies = {}, {}

    def probs_of(g, a):
        at = slice(a * lot, (a + 1) * lot)
        for b in range(PACK):
            ab = slice(a * lot + b * rows, a * lot + (b + 1) * rows)
            s = nt(keys[g], heads(q_vm, g, a, b)) * scale
            s = jnp.where(allowed, s, -jnp.inf)
            e = jnp.exp(s - jnp.max(s, axis=0, keepdims=True))
            p = e * (1.0 / jnp.sum(e, axis=0, keepdims=True))
            p_f32[g, ab, :] = p
            p_send[g, ab, :] = p.astype(BF16)
        if (g, a) != RAW:
            c = remote(
                p_send.at[g, at], p_recv.at[g, at], p_ss.at[g, a], p_rs.at[g, a], dev(up, me)
            )
            c.start()
            p_copies[g, a] = c

    def dprobs_of(g, a, values):
        at = slice(a * lot, (a + 1) * lot)
        for b in range(PACK):
            ab = slice(a * lot + b * rows, a * lot + (b + 1) * rows)
            dp = nt(values, heads(c_vm, g, a, b))
            dp = dp - jnp.sum(dp, axis=0, keepdims=True) * (1.0 / rows)
            dp_send[g, ab, :] = dp.astype(BF16)
        c = remote(
            dp_send.at[g, at], dp_recv.at[g, at], dp_ss.at[g, a], dp_rs.at[g, a], dev(down, me)
        )
        c.start()
        dp_copies[g, a] = c

    @pl.when(sec < last)
    def _():
        pl.semaphore_wait(ready_up, 1)

    first = [c for c in chunks if c != RAW]
    probs_of(*first[0])
    assemble(1)
    v_own[...] = asm[1].astype(BF16)
    v_copy = remote(v_own, v_up, v_sem.at[0], v_sem.at[1], dev(up, me))
    v_copy.start()
    for c in first[1:]:
        probs_of(*c)

    @pl.when(sec == 0)
    def _():
        pl.semaphore_wait(ready_down, 1)
        raw.start()

    probs_of(*RAW)

    loads[1].wait()
    v_copy.wait_recv()
    for g, a in first:
        dprobs_of(g, a, v_up[:, g * D : (g + 1) * D])

    for g in range(groups):
        values = v_own[:, g * D : (g + 1) * D]
        for b in range(PACK):
            k_bd[g, b * rows : (b + 1) * rows, b * D : (b + 1) * D] = keys[g]
            v_bd[g, b * rows : (b + 1) * rows, b * D : (b + 1) * D] = values
    for g, a in chunks:
        at = (g * lots + a) * wide
        o = tn(p_send[g, a * lot : (a + 1) * lot, :], v_bd[g])
        att_vm[0, :, at : at + wide] = o.astype(BF16)

    def dscores_of(g, a, dprobs):
        ds_list = []
        dk = None
        for b in range(PACK):
            p = p_f32[g, a * lot + b * rows : a * lot + (b + 1) * rows, :]
            dp = dprobs(b)
            delta = jnp.sum(p * dp, axis=0, keepdims=True)
            ds = (p * (dp - delta)).astype(BF16)
            ds_list.append(ds)
            t = nn(ds, heads(q_vm, g, a, b))
            dk = t if dk is None else dk + t
        return jnp.concatenate(ds_list, axis=0), dk

    def grad_queries_of(g, a, ds):
        at = (g * lots + a) * wide
        gq_vm[0, :, at : at + wide] = (tn(ds, k_bd[g]) * scale).astype(BF16)

    raw.wait_recv()
    g, a = RAW
    raw_ds, raw_dk = dscores_of(
        g, a, lambda b: nt(v_own[:, g * D : (g + 1) * D], raw_vm[:, b * D : (b + 1) * D])
    )
    raw_dv = None
    for b in range(PACK):
        t = nn(
            p_send[g, a * lot + b * rows : a * lot + (b + 1) * rows, :],
            raw_vm[:, b * D : (b + 1) * D],
        )
        raw_dv = t if raw_dv is None else raw_dv + t
    rv_t[...] = raw_dv
    grad_queries_of(g, a, raw_ds)

    rest = []

    def piece(ref, to):
        return ref.at[pl.ds(pl.multiple_of(to * share, share), share), :]

    for d in range(1, nseq):
        to = lax.rem(seq + d, nseq)
        c = remote(
            piece(rv_t, to), rv_r.at[d], rv_ss.at[d], rv_rs.at[d],
            {"section": sec, "seq": to, "tp": tp},
        )
        c.start()
        rest.append(c)

    for g in range(groups):
        dv = None
        for a in range(lots):
            if (g, a) == RAW:
                continue
            p_copies[g, a].wait_recv()
            for b in range(PACK):
                t = nn(
                    p_recv[g, a * lot + b * rows : a * lot + (b + 1) * rows, :],
                    heads(c_vm, g, a, b),
                )
                dv = t if dv is None else dv + t
        for q in range(nseq):
            dv_t[q, g] = dv[q * share : (q + 1) * share].astype(BF16)
        for d in range(nseq):
            to = lax.rem(seq + d, nseq)
            c = remote(
                dv_t.at[to, g], dv_r.at[d, g], dv_ss.at[g, d], dv_rs.at[g, d],
                {"section": down, "seq": to, "tp": tp},
            )
            c.start()
            rest.append(c)

    for g in range(groups):
        dk = None
        done = []
        for a in range(lots):
            if (g, a) == RAW:
                dk = raw_dk
                continue
            dp_copies[g, a].wait_recv()
            at = a * lot
            ds, t = dscores_of(
                g, a, lambda b: dp_recv[g, at + b * rows : at + (b + 1) * rows, :].astype(F32)
            )
            dk = t if dk is None else dk + t
            done.append((a, ds))
        dk_t[g] = dk * scale
        for d in range(1, nseq):
            to = lax.rem(seq + d, nseq)
            c = remote(
                piece(dk_t.at[g], to), dk_r.at[d, g], dk_ss.at[g, d], dk_rs.at[g, d],
                {"section": sec, "seq": to, "tp": tp},
            )
            c.start()
            rest.append(c)
        for a, ds in done:
            grad_queries_of(g, a, ds)

    for c in rest:
        c.wait_recv()
    here = pl.ds(pl.multiple_of(seq * share, share), share)
    for g in range(groups):
        dk = dk_t[g, here, :]
        for d in range(1, nseq):
            dk = dk + dk_r[d, g]
        dv = dv_r[0, g].astype(F32)
        for d in range(1, nseq):
            dv = dv + dv_r[d, g].astype(F32)
        if g == RAW[0]:
            dv = dv + rv_t[here, :]
            for d in range(1, nseq):
                dv = dv + rv_r[d]
        gk_out[0, :, g * D : (g + 1) * D] = dk.astype(BF16)
        gv_out[0, :, g * D : (g + 1) * D] = dv.astype(BF16)
    for c in kv_copies + [raw, v_copy] + list(p_copies.values()) + list(dp_copies.values()) + rest:
        c.wait_send()


def put_out(*refs):
    sems = refs[8]
    copies = []
    for i in range(4):
        step = refs[i].shape[1] // CUTS if i < 2 else refs[i].shape[1]
        for j in range(refs[i].shape[1] // step):
            at = slice(j * step, (j + 1) * step)
            copies.append(
                pltpu.make_async_copy(refs[i].at[:, at], refs[4 + i].at[:, at], sems.at[i, j])
            )
    for c in copies:
        c.start()
    for c in copies:
        c.wait()


def per_device(nsec, nseq, ntp, queries, keys, values, cotangent, pattern, tile_owner):
    n = nseq * ntp
    part = keys.shape[1]
    width = keys.shape[2] // ntp
    rows = part * n
    groups = width // HEAD_SIZE
    text, cols = queries.shape[1:]
    share = rows // nseq
    lots = FAN // PACK
    D = HEAD_SIZE
    dma = pltpu.SemaphoreType.DMA
    vm = pltpu.VMEM
    anyspace = pl.BlockSpec(memory_space=pl.ANY)
    smem = pl.BlockSpec(memory_space=pltpu.SMEM)
    vmem = pl.BlockSpec(memory_space=pltpu.VMEM)
    results = pl.pallas_call(
        functools.partial(kernel, nsec, nseq, ntp),
        out_shape=(
            vm((1, text, cols), BF16),
            vm((1, text, cols), BF16),
            vm((1, share, width), BF16),
            vm((1, share, width), BF16),
        ),
        in_specs=[anyspace] * 4 + [smem] * 2,
        out_specs=(vmem,) * 4,
        scratch_shapes=[
            vm((text, cols), BF16),
            vm((text, cols), BF16),
            vm((text, PACK * D), BF16),
            vm((ntp, 2, part, width), BF16),
            vm((n, 2, part, width), BF16),
            vm((2, rows, width), F32),
            vm((rows, width), BF16),
            vm((rows, width), BF16),
            vm((groups, PACK * rows, PACK * D), BF16),
            vm((groups, PACK * rows, PACK * D), BF16),
            vm((groups, FAN * rows, text), F32),
            vm((groups, FAN * rows, text), BF16),
            vm((groups, FAN * rows, text), BF16),
            vm((groups, FAN * rows, text), BF16),
            vm((groups, FAN * rows, text), BF16),
            vm((groups, rows, D), F32),
            vm((nseq, groups, share, D), F32),
            vm((nseq, groups, share, D), BF16),
            vm((nseq, groups, share, D), BF16),
            vm((rows, D), F32),
            vm((nseq, share, D), F32),
            dma((2,)), dma((ntp, 2)), dma((1,)),
            dma((n,)), dma((n,)), dma((2,)), dma((2,)),
            dma((groups, lots)), dma((groups, lots)), dma((groups, lots)), dma((groups, lots)),
            dma((groups, nseq)), dma((groups, nseq)), dma((groups, nseq)), dma((groups, nseq)),
            dma((nseq,)), dma((nseq,)),
            pltpu.SemaphoreType.REGULAR, pltpu.SemaphoreType.REGULAR,
        ],
        compiler_params=pltpu.CompilerParams(collective_id=0, has_side_effects=True),
        name="cross",
    )(queries, keys, values, cotangent, pattern, tile_owner)
    return pl.pallas_call(
        put_out,
        out_shape=tuple(jax.ShapeDtypeStruct(r.shape, r.dtype) for r in results),
        in_specs=[vmem] * 4,
        out_specs=(anyspace,) * 4,
        scratch_shapes=[dma((4, CUTS))],
        name="put",
    )(*[pltpu.with_memory_space_constraint(r, pltpu.VMEM) for r in results])


def solution(mesh):
    nsec, nseq, ntp = (mesh.shape[a] for a in ("section", "seq", "tp"))
    in_specs = (
        P("section", "seq", "tp"),
        P("section", ("seq", "tp"), None),
        P("section", ("seq", "tp"), None),
        P("section", "seq", "tp"),
        P("section", "seq", None),
        P("section", None),
    )
    out_specs = (P("section", "seq", "tp"),) * 4
    return jax.shard_map(
        functools.partial(per_device, nsec, nseq, ntp),
        mesh=mesh, in_specs=in_specs, out_specs=out_specs, check_vma=False,
    )
```

```python
import functools

import jax
import jax.numpy as jnp
from jax import lax
from jax.experimental import pallas as pl
from jax.experimental.pallas import tpu as pltpu
from jax.sharding import PartitionSpec as P

QUERY_HEADS = 64
KEY_VALUE_HEADS = 8
HEAD_SIZE = 128
FAN = QUERY_HEADS // KEY_VALUE_HEADS
PACK = 4
CUTS = 4
RAW = 1
AHEAD = 2
SPLIT = 3
MESH = pl.DeviceIdType.MESH
F32 = jnp.float32
BF16 = jnp.bfloat16


def nt(a, b):
    return lax.dot_general(a, b, (((1,), (1,)), ((), ())), preferred_element_type=F32)


def nn(a, b):
    return lax.dot_general(a, b, (((1,), (0,)), ((), ())), preferred_element_type=F32)


def tn(a, b):
    return lax.dot_general(a, b, (((0,), (0,)), ((), ())), preferred_element_type=F32)


def cut(j, size=HEAD_SIZE):
    return pl.ds(pl.multiple_of(j * size, size), size)


def kernel(
    nsec, nseq, ntp,
    q_hbm, k_hbm, v_hbm, c_hbm, pat, own,
    att_vm, gq_vm, gk_out, gv_out,
    q_vm, c_vm, raw_vm,
    gath, asm, kvs,
    k_bd, v_bd,
    p_f32, p_send, p_recv, dp_send, dp_recv,
    dk_t, dk_r, dv_acc, dv_t, dv_r, rv_t, rv_r,
    load_sem, own_sem, kv_ss, kv_rs, raw_sem,
    p_ss, p_rs, dp_ss, dp_rs, sum_ss, sum_rs,
    ready_up, ready_down,
):
    scale = HEAD_SIZE ** (-0.5)
    D = HEAD_SIZE
    n = nseq * ntp
    text, cols = q_vm.shape
    part = k_hbm.shape[1]
    width = k_hbm.shape[2] // ntp
    rows = part * n
    groups = width // D
    share = rows // nseq
    lots = FAN // PACK
    lot = PACK * rows
    wide = PACK * D
    nch = groups * lots
    sec, seq, tp = lax.axis_index("section"), lax.axis_index("seq"), lax.axis_index("tp")
    me = seq * ntp + tp
    up, down = lax.rem(sec + 1, nsec), lax.rem(sec + nsec - 1, nsec)
    last = nsec - 1
    inner = (sec > 0) & (sec < last)

    def dev(s, i):
        return {"section": s, "seq": lax.div(i, ntp), "tp": lax.rem(i, ntp)}

    def signal(sem, to):
        pl.semaphore_signal(sem, inc=1, device_id=to, device_id_type=MESH)

    def remote(src, dst, ss, rs, to):
        return pltpu.make_async_remote_copy(
            src_ref=src, dst_ref=dst, send_sem=ss, recv_sem=rs, device_id=to, device_id_type=MESH
        )

    def same(s=sec):
        return {"section": s, "seq": seq, "tp": tp}

    barrier = pltpu.get_barrier_semaphore()

    @pl.loop(1, n)
    def _(d):
        signal(barrier, dev(sec, lax.rem(me + n - d, n)))

    @pl.when(sec < last)
    def _():
        signal(barrier, same(up))

    @pl.when(sec == 0)
    def _():
        @pl.loop(0, n)
        def _(d):
            signal(barrier, dev(down, lax.rem(me + d, n)))

    def half(ref, i):
        return ref.at[0, :, cut(lax.rem(i, ntp), width)]

    mine = [
        pltpu.make_async_copy(half(k_hbm, me), gath.at[0, me], own_sem.at[0]),
        pltpu.make_async_copy(half(v_hbm, me), gath.at[1, me], own_sem.at[1]),
    ]
    loads = [
        pltpu.make_async_copy(q_hbm.at[0], q_vm, load_sem.at[0]),
        pltpu.make_async_copy(c_hbm.at[0], c_vm, load_sem.at[1]),
    ]
    for c in mine + loads:
        c.start()

    from_others = jnp.where(sec > 0, 1, 0) + jnp.where(sec == last, n, 0)
    pl.semaphore_wait(barrier, n - 1 + from_others)

    @pl.when(sec > 0)
    def _():
        signal(ready_up, same(down))

    @pl.when(sec == last)
    def _():
        signal(ready_down, same(up))

    def gather(which, ref, to, d):
        peer = lax.rem(me + n - d, n)
        return remote(
            half(ref, peer), gath.at[which, me], kv_ss.at[which], kv_rs.at[which], dev(to, peer)
        )

    def gathered(which, count):
        return remote(
            gath.at[which, 0:count], gath.at[which, 0:count],
            kv_ss.at[which], kv_rs.at[which], same(),
        )

    @pl.loop(1, n)
    def _(d):
        gather(0, k_hbm, sec, d).start()

    raw = remote(
        c_hbm.at[0, :, 0 : RAW * wide], raw_vm, raw_sem.at[0], raw_sem.at[1], same(down)
    )

    @pl.when(inner)
    def _():
        raw.start()

    @pl.when(sec < last)
    def _():
        pl.semaphore_wait(ready_up, 1)

    @pl.loop(0, n)
    def _(d):
        gather(2, v_hbm, up, d).start()

    @pl.when(sec == last)
    def _():
        raw.start()

    @pl.loop(1, n)
    def _(d):
        gather(1, v_hbm, sec, d).start()

    row_tile = lax.broadcasted_iota(jnp.int32, (rows, text), 0) // (rows // own.shape[1])
    blocks = pat.shape[1]
    lane_block = lax.broadcasted_iota(jnp.int32, (rows, text), 1) // (text // blocks)
    allowed = jnp.zeros((rows, text), jnp.bool_)
    for b in range(blocks):
        for t in range(own.shape[1]):
            owner = jnp.where(pat[0, b, t] > 0, own[0, t], -1)
            hit = row_tile == owner
            if blocks > 1:
                hit = hit & (lane_block == b)
            allowed = allowed | hit
    k_bd[...] = jnp.zeros_like(k_bd)
    v_bd[...] = jnp.zeros_like(v_bd)

    def assemble(which):
        for i in range(n):
            asm[which, part * i : part * (i + 1), :] = gath[which, i].astype(F32)
        kvs[which] = asm[which].astype(BF16)

    def lines(b):
        return slice(b * rows, (b + 1) * rows)

    def probs_copy(c):
        return remote(p_send.at[c], p_recv.at[c], p_ss, p_rs.at[c], same(up))

    def dprobs_copy(c):
        return remote(dp_send.at[c], dp_recv.at[c], dp_ss, dp_rs.at[c], same(down))

    def probs_of(c):
        key = kvs[0, :, cut(lax.div(c, lots))]
        for b in range(PACK):
            s = nt(key, q_vm[:, cut(c * PACK + b)]) * scale
            s = jnp.where(allowed, s, -jnp.inf)
            e = jnp.exp(s - jnp.max(s, axis=0, keepdims=True))
            p = e * (1.0 / jnp.sum(e, axis=0, keepdims=True))
            p_f32[c, lines(b), :] = p
            p_send[c, lines(b), :] = p.astype(BF16)

        @pl.when((c >= RAW) | (sec == last))
        def _():
            probs_copy(c).start()

    def centred(value, block):
        dp = nt(value, block)
        return (dp - jnp.sum(dp, axis=0, keepdims=True) * (1.0 / rows)).astype(BF16)

    def dprobs_of(c):
        value = kvs[2, :, cut(lax.div(c, lots))]
        for b in range(PACK):
            dp_send[c, lines(b), :] = centred(value, c_vm[:, cut(c * PACK + b)])
        dprobs_copy(c).start()

    mine[0].wait()
    gathered(0, n - 1).wait_recv()
    assemble(0)
    loads[0].wait()
    ahead = jnp.where(sec == 0, nch, jnp.where(sec == last, RAW + SPLIT, RAW + AHEAD))

    @pl.loop(0, ahead)
    def _(c):
        probs_of(c)

    mine[1].wait()
    gathered(1, n - 1).wait_recv()
    assemble(1)
    loads[1].wait()

    def attend():
        @pl.loop(0, groups)
        def _(g):
            key, value = kvs[0, :, cut(g)], kvs[1, :, cut(g)]
            for b in range(PACK):
                k_bd[g, lines(b), b * D : (b + 1) * D] = key
                v_bd[g, lines(b), b * D : (b + 1) * D] = value
            for a in range(lots):
                c = g * lots + a
                att_vm[0, :, cut(c, wide)] = tn(p_send[c], v_bd[g]).astype(BF16)

    @pl.when(sec == 0)
    def _():
        pl.semaphore_wait(ready_down, 1)
        raw.wait_recv()

    gathered(2, n).wait_recv()
    assemble(2)

    @pl.loop(jnp.where(sec == 0, 0, RAW), jnp.where(sec == last, nch + nch - ahead, nch))
    def _(i):
        @pl.when(i < nch)
        def _():
            dprobs_of(i)

        c = jnp.where(sec == last, i - nch, i - RAW) + ahead

        @pl.when((inner & (c < nch)) | (i >= nch))
        def _():
            probs_of(c)

    attend()

    def grad_values_of(probs, c, block):
        dv = None
        for b in range(PACK):
            t = nn(probs[c, lines(b), :], block(b))
            dv = t if dv is None else dv + t
        return dv

    def spread(src, dst, which, to_sec, first):
        for d in range(first, nseq):
            to = lax.rem(seq + d, nseq)
            remote(
                src(to), dst(d), sum_ss.at[which], sum_rs.at[which],
                {"section": to_sec, "seq": to, "tp": tp},
            ).start()

    @pl.when(inner)
    def _():
        raw.wait_recv()

    @pl.when(sec < last)
    def _():
        for c in range(RAW):
            value = kvs[1, :, cut(c // lots)]

            def block(b):
                j = c * PACK + b
                return raw_vm[:, j * D : (j + 1) * D]

            for b in range(PACK):
                dp_recv[c, lines(b), :] = centred(value, block(b))
            dv = grad_values_of(p_send, c, block)
            for q in range(nseq):
                rv_t[q, c] = dv[q * share : (q + 1) * share]
        spread(lambda to: rv_t.at[to], lambda d: rv_r.at[d], 2, sec, 1)

    @pl.when(sec == last)
    def _():
        rv_t[...] = jnp.zeros_like(rv_t)
        rv_r[...] = jnp.zeros_like(rv_r)

    def value_step(g):
        dv_acc[...] = jnp.zeros_like(dv_acc)
        for a in range(lots):
            c = g * lots + a

            @pl.when((c >= RAW) | (sec == 0))
            def _():
                probs_copy(c).wait_recv()
                dv_acc[...] += grad_values_of(p_recv, c, lambda b: c_vm[:, cut(c * PACK + b)])

        for q in range(nseq):
            dv_t[q, g] = dv_acc[q * share : (q + 1) * share].astype(BF16)
        spread(lambda to: dv_t.at[to, g], lambda d: dv_r.at[d, g], 1, down, 0)

    def key_step(g):
        dk = None
        done = []
        for a in range(lots):
            c = g * lots + a

            @pl.when((c >= RAW) | (sec == last))
            def _():
                dprobs_copy(c).wait_recv()

            ds_list = []
            for b in range(PACK):
                p = p_f32[c, lines(b), :]
                dp = dp_recv[c, lines(b), :].astype(F32)
                delta = jnp.sum(p * dp, axis=0, keepdims=True)
                ds = (p * (dp - delta)).astype(BF16)
                ds_list.append(ds)
                t = nn(ds, q_vm[:, cut(c * PACK + b)])
                dk = t if dk is None else dk + t
            done.append((c, jnp.concatenate(ds_list, axis=0)))
        dk = dk * scale
        for q in range(nseq):
            dk_t[q, g] = dk[q * share : (q + 1) * share]
        spread(lambda to: dk_t.at[to, g], lambda d: dk_r.at[d, g], 0, sec, 1)
        for c, ds in done:
            gq_vm[0, :, cut(c, wide)] = (tn(ds, k_bd[g]) * scale).astype(BF16)

    @pl.loop(0, 2 * groups)
    def _(i):
        g = lax.rem(i, groups)
        values_now = (i < groups) == (sec > 0)

        @pl.when(values_now)
        def _():
            value_step(g)

        @pl.when(jnp.logical_not(values_now))
        def _():
            key_step(g)

    def whole(src, dst, which):
        return remote(src, dst, sum_ss.at[which], sum_rs.at[which], same())

    dk_all = whole(dk_t.at[1:], dk_r.at[1:], 0)
    dv_all = whole(dv_t, dv_r, 1)
    rv_all = whole(rv_t.at[1:], rv_r.at[1:], 2)

    @pl.when(sec < last)
    def _():
        rv_all.wait_recv()

    dk_all.wait_recv()
    dv_all.wait_recv()
    for g in range(groups):
        dk = dk_t[seq, g]
        for d in range(1, nseq):
            dk = dk + dk_r[d, g]
        dv = dv_r[0, g].astype(F32)
        for d in range(1, nseq):
            dv = dv + dv_r[d, g].astype(F32)
        for c in range(RAW):
            if c // lots == g:
                dv = dv + rv_t[seq, c]
                for d in range(1, nseq):
                    dv = dv + rv_r[d, c]
        gk_out[0, :, g * D : (g + 1) * D] = dk.astype(BF16)
        gv_out[0, :, g * D : (g + 1) * D] = dv.astype(BF16)

    gathered(0, n - 1).wait_send()
    gathered(1, n - 1).wait_send()
    gathered(2, n).wait_send()
    dk_all.wait_send()
    dv_all.wait_send()

    def sent(ref, ss, everything):
        for first, where in ((0, everything), (RAW, jnp.logical_not(everything))):

            @pl.when(where)
            def _():
                part = ref.at[first:]
                remote(part, part, ss, raw_sem.at[1], same()).wait_send()

    sent(p_send, p_ss, sec == last)
    sent(dp_send, dp_ss, sec == 0)

    @pl.when(sec > 0)
    def _():
        raw.wait_send()

    @pl.when(sec < last)
    def _():
        rv_all.wait_send()


def put_out(*refs):
    sems = refs[8]
    copies = []
    for i in range(4):
        step = refs[i].shape[1] // CUTS if i < 2 else refs[i].shape[1]
        for j in range(refs[i].shape[1] // step):
            at = slice(j * step, (j + 1) * step)
            copies.append(
                pltpu.make_async_copy(refs[i].at[:, at], refs[4 + i].at[:, at], sems.at[i, j])
            )
    for c in copies:
        c.start()
    for c in copies:
        c.wait()


def per_device(nsec, nseq, ntp, queries, keys, values, cotangent, pattern, tile_owner):
    n = nseq * ntp
    part = keys.shape[1]
    width = keys.shape[2] // ntp
    rows = part * n
    groups = width // HEAD_SIZE
    text, cols = queries.shape[1:]
    share = rows // nseq
    nch = groups * (FAN // PACK)
    D = HEAD_SIZE
    dma = pltpu.SemaphoreType.DMA
    vm = pltpu.VMEM
    anyspace = pl.BlockSpec(memory_space=pl.ANY)
    smem = pl.BlockSpec(memory_space=pltpu.SMEM)
    vmem = pl.BlockSpec(memory_space=pltpu.VMEM)
    results = pl.pallas_call(
        functools.partial(kernel, nsec, nseq, ntp),
        out_shape=(
            vm((1, text, cols), BF16),
            vm((1, text, cols), BF16),
            vm((1, share, width), BF16),
            vm((1, share, width), BF16),
        ),
        in_specs=[anyspace] * 4 + [smem] * 2,
        out_specs=(vmem,) * 4,
        scratch_shapes=[
            vm((text, cols), BF16),
            vm((text, cols), BF16),
            vm((text, RAW * PACK * D), BF16),
            vm((3, n, part, width), BF16),
            vm((3, rows, width), F32),
            vm((3, rows, width), BF16),
            vm((groups, PACK * rows, PACK * D), BF16),
            vm((groups, PACK * rows, PACK * D), BF16),
            vm((nch, PACK * rows, text), F32),
            vm((nch, PACK * rows, text), BF16),
            vm((nch, PACK * rows, text), BF16),
            vm((nch, PACK * rows, text), BF16),
            vm((nch, PACK * rows, text), BF16),
            vm((nseq, groups, share, D), F32),
            vm((nseq, groups, share, D), F32),
            vm((rows, D), F32),
            vm((nseq, groups, share, D), BF16),
            vm((nseq, groups, share, D), BF16),
            vm((nseq, RAW, share, D), F32),
            vm((nseq, RAW, share, D), F32),
            dma((2,)), dma((2,)), dma((3,)), dma((3,)), dma((2,)),
            dma, dma((nch,)), dma, dma((nch,)), dma((3,)), dma((3,)),
            pltpu.SemaphoreType.REGULAR, pltpu.SemaphoreType.REGULAR,
        ],
        compiler_params=pltpu.CompilerParams(collective_id=0, has_side_effects=True),
        name="cross",
    )(queries, keys, values, cotangent, pattern, tile_owner)
    return pl.pallas_call(
        put_out,
        out_shape=tuple(jax.ShapeDtypeStruct(r.shape, r.dtype) for r in results),
        in_specs=[vmem] * 4,
        out_specs=(anyspace,) * 4,
        scratch_shapes=[dma((4, CUTS))],
        name="put",
    )(*[pltpu.with_memory_space_constraint(r, pltpu.VMEM) for r in results])


def solution(mesh):
    nsec, nseq, ntp = (mesh.shape[a] for a in ("section", "seq", "tp"))
    in_specs = (
        P("section", "seq", "tp"),
        P("section", ("seq", "tp"), None),
        P("section", ("seq", "tp"), None),
        P("section", "seq", "tp"),
        P("section", "seq", None),
        P("section", None),
    )
    out_specs = (P("section", "seq", "tp"),) * 4
    return jax.shard_map(
        functools.partial(per_device, nsec, nseq, ntp),
        mesh=mesh, in_specs=in_specs, out_specs=out_specs, check_vma=False,
    )
```

```python
import functools

import jax
import jax.numpy as jnp
from jax import lax
from jax.experimental import pallas as pl
from jax.experimental.pallas import tpu as pltpu
from jax.sharding import PartitionSpec as P

QUERY_HEADS = 64
KEY_VALUE_HEADS = 8
HEAD_SIZE = 128
FAN = QUERY_HEADS // KEY_VALUE_HEADS
PACK = 4
CUTS = 4
RAW = 1
AHEAD = 2
SPLIT = 3
LATER = 4
START = 0
MESH = pl.DeviceIdType.MESH
F32 = jnp.float32
BF16 = jnp.bfloat16


def nt(a, b):
    return lax.dot_general(a, b, (((1,), (1,)), ((), ())), preferred_element_type=F32)


def nn(a, b):
    return lax.dot_general(a, b, (((1,), (0,)), ((), ())), preferred_element_type=F32)


def tn(a, b):
    return lax.dot_general(a, b, (((0,), (0,)), ((), ())), preferred_element_type=F32)


def cut(j, size=HEAD_SIZE):
    return pl.ds(pl.multiple_of(j * size, size), size)


def kernel(
    nsec, nseq, ntp,
    q_hbm, k_hbm, v_hbm, c_hbm, pat, own,
    att_vm, gq_vm, gk_out, gv_out,
    q_vm, c_vm, raw_vm,
    gath, asm, kvs,
    k_bd, v_bd,
    p_f32, p_send, p_recv, dp_send, dp_recv,
    dk_t, dk_r, dv_acc, dv_t, dv_r, rv_t, rv_r,
    load_sem, own_sem, kv_ss, kv_rs, raw_sem,
    p_ss, p_rs, dp_ss, dp_rs, sum_ss, sum_rs,
    ready_up, ready_down,
):
    scale = HEAD_SIZE ** (-0.5)
    D = HEAD_SIZE
    n = nseq * ntp
    text, cols = q_vm.shape
    part = k_hbm.shape[1]
    width = k_hbm.shape[2] // ntp
    rows = part * n
    groups = width // D
    share = rows // nseq
    lots = FAN // PACK
    lot = PACK * rows
    wide = PACK * D
    nch = groups * lots
    sec, seq, tp = lax.axis_index("section"), lax.axis_index("seq"), lax.axis_index("tp")
    me = seq * ntp + tp
    up, down = lax.rem(sec + 1, nsec), lax.rem(sec + nsec - 1, nsec)
    last = nsec - 1
    inner = (sec > 0) & (sec < last)
    raw_in, raw_out = sec >= 0, sec >= 0
    whole_in, whole_out = jnp.logical_not(raw_in), jnp.logical_not(raw_out)

    def dev(s, i):
        return {"section": s, "seq": lax.div(i, ntp), "tp": lax.rem(i, ntp)}

    def signal(sem, to):
        pl.semaphore_signal(sem, inc=1, device_id=to, device_id_type=MESH)

    def remote(src, dst, ss, rs, to):
        return pltpu.make_async_remote_copy(
            src_ref=src, dst_ref=dst, send_sem=ss, recv_sem=rs, device_id=to, device_id_type=MESH
        )

    def same(s=sec):
        return {"section": s, "seq": seq, "tp": tp}

    barrier = pltpu.get_barrier_semaphore()

    @pl.loop(1, n)
    def _(d):
        signal(barrier, dev(sec, lax.rem(me + n - d, n)))

    @pl.when(sec < last)
    def _():
        signal(barrier, same(up))

    @pl.when(sec == 0)
    def _():
        @pl.loop(0, n)
        def _(d):
            signal(barrier, dev(down, lax.rem(me + d, n)))

    def half(ref, i):
        return ref.at[0, :, cut(lax.rem(i, ntp), width)]

    mine = [
        pltpu.make_async_copy(half(k_hbm, me), gath.at[0, me], own_sem.at[0]),
        pltpu.make_async_copy(half(v_hbm, me), gath.at[1, me], own_sem.at[1]),
    ]
    loads = [
        pltpu.make_async_copy(q_hbm.at[0], q_vm, load_sem.at[0]),
        pltpu.make_async_copy(c_hbm.at[0], c_vm, load_sem.at[1]),
    ]
    for c in mine + loads:
        c.start()

    from_others = jnp.where(sec > 0, 1, 0) + jnp.where(sec == last, n, 0)
    pl.semaphore_wait(barrier, n - 1 + from_others)

    @pl.when(sec > 0)
    def _():
        signal(ready_up, same(down))

    @pl.when(sec == last)
    def _():
        signal(ready_down, same(up))

    def gather(which, ref, to, d):
        peer = lax.rem(me + n - d, n)
        return remote(
            half(ref, peer), gath.at[which, me], kv_ss.at[which], kv_rs.at[which], dev(to, peer)
        )

    def gathered(which, count):
        return remote(
            gath.at[which, 0:count], gath.at[which, 0:count],
            kv_ss.at[which], kv_rs.at[which], same(),
        )

    @pl.loop(1, n)
    def _(d):
        gather(0, k_hbm, sec, d).start()

    raw = remote(
        c_hbm.at[0, :, 0 : RAW * wide], raw_vm, raw_sem.at[0], raw_sem.at[1], same(down)
    )

    @pl.when(inner & raw_out)
    def _():
        raw.start()

    @pl.when(sec < last)
    def _():
        pl.semaphore_wait(ready_up, 1)

    @pl.loop(0, n)
    def _(d):
        gather(2, v_hbm, up, d).start()

    @pl.when((sec == last) & raw_out)
    def _():
        raw.start()

    @pl.loop(1, n)
    def _(d):
        gather(1, v_hbm, sec, d).start()

    row_tile = lax.broadcasted_iota(jnp.int32, (rows, text), 0) // (rows // own.shape[1])
    blocks = pat.shape[1]
    lane_block = lax.broadcasted_iota(jnp.int32, (rows, text), 1) // (text // blocks)
    allowed = jnp.zeros((rows, text), jnp.bool_)
    for b in range(blocks):
        for t in range(own.shape[1]):
            owner = jnp.where(pat[0, b, t] > 0, own[0, t], -1)
            hit = row_tile == owner
            if blocks > 1:
                hit = hit & (lane_block == b)
            allowed = allowed | hit
    k_bd[...] = jnp.zeros_like(k_bd)
    v_bd[...] = jnp.zeros_like(v_bd)

    def assemble(which):
        for i in range(n):
            asm[which, part * i : part * (i + 1), :] = gath[which, i].astype(F32)
        kvs[which] = asm[which].astype(BF16)

    def lines(b):
        return slice(b * rows, (b + 1) * rows)

    def probs_copy(c):
        return remote(p_send.at[c], p_recv.at[c], p_ss, p_rs.at[c], same(up))

    def dprobs_copy(c):
        return remote(dp_send.at[c], dp_recv.at[c], dp_ss, dp_rs.at[c], same(down))

    def probs_of(c):
        key = kvs[0, :, cut(lax.div(c, lots))]
        for b in range(PACK):
            s = nt(key, q_vm[:, cut(c * PACK + b)]) * scale
            s = jnp.where(allowed, s, -jnp.inf)
            e = jnp.exp(s - jnp.max(s, axis=0, keepdims=True))
            p = e * (1.0 / jnp.sum(e, axis=0, keepdims=True))
            p_f32[c, lines(b), :] = p
            p_send[c, lines(b), :] = p.astype(BF16)

        @pl.when((c >= RAW) | whole_in)
        def _():
            probs_copy(c).start()

    def centred(value, block):
        dp = nt(value, block)
        return (dp - jnp.sum(dp, axis=0, keepdims=True) * (1.0 / rows)).astype(BF16)

    def dprobs_of(c):
        value = kvs[2, :, cut(lax.div(c, lots))]
        for b in range(PACK):
            dp_send[c, lines(b), :] = centred(value, c_vm[:, cut(c * PACK + b)])
        dprobs_copy(c).start()

    mine[0].wait()
    gathered(0, n - 1).wait_recv()
    assemble(0)
    loads[0].wait()

    @pl.when(sec == 0)
    def _():
        pl.semaphore_wait(ready_down, 1)
        raw.start()

    ahead = jnp.where(sec == 0, nch, jnp.where(sec == last, RAW + SPLIT, RAW + AHEAD))

    @pl.loop(0, ahead)
    def _(c):
        probs_of(c)

    mine[1].wait()
    gathered(1, n - 1).wait_recv()
    assemble(1)
    loads[1].wait()

    def attend():
        @pl.loop(0, groups)
        def _(g):
            key, value = kvs[0, :, cut(g)], kvs[1, :, cut(g)]
            for b in range(PACK):
                k_bd[g, lines(b), b * D : (b + 1) * D] = key
                v_bd[g, lines(b), b * D : (b + 1) * D] = value
            for a in range(lots):
                c = g * lots + a
                att_vm[0, :, cut(c, wide)] = tn(p_send[c], v_bd[g]).astype(BF16)

    @pl.when(sec == 0)
    def _():
        attend()

    gathered(2, n).wait_recv()
    assemble(2)

    lowest = jnp.where(whole_out, 0, RAW)

    @pl.loop(lowest, jnp.where(sec == last, nch + nch - ahead, nch))
    def _(i):
        @pl.when(i < nch)
        def _():
            dprobs_of(i)

        c = jnp.where(sec == last, i - nch, i - lowest) + ahead

        @pl.when((inner & (c < nch)) | (i >= nch))
        def _():
            probs_of(c)

    @pl.when(sec > 0)
    def _():
        attend()

    def grad_values_of(probs, c, block):
        dv = None
        for b in range(PACK):
            t = nn(probs[c, lines(b), :], block(b))
            dv = t if dv is None else dv + t
        return dv

    def spread(src, dst, which, to_sec, first):
        for d in range(first, nseq):
            to = lax.rem(seq + d, nseq)
            remote(
                src(to), dst(d), sum_ss.at[which], sum_rs.at[which],
                {"section": to_sec, "seq": to, "tp": tp},
            ).start()

    @pl.when(raw_in)
    def _():
        raw.wait_recv()
        for c in range(RAW):
            value = kvs[1, :, cut(c // lots)]

            def block(b):
                j = c * PACK + b
                return raw_vm[:, j * D : (j + 1) * D]

            for b in range(PACK):
                dp_recv[c, lines(b), :] = centred(value, block(b))
            dv = grad_values_of(p_send, c, block)
            for q in range(nseq):
                rv_t[q, c] = dv[q * share : (q + 1) * share]
        spread(lambda to: rv_t.at[to], lambda d: rv_r.at[d], 2, sec, 1)

    @pl.when(whole_in)
    def _():
        rv_t[...] = jnp.zeros_like(rv_t)
        rv_r[...] = jnp.zeros_like(rv_r)

    def value_step(g):
        dv_acc[...] = jnp.zeros_like(dv_acc)
        for a in range(lots):
            c = g * lots + a

            @pl.when((c >= RAW) | whole_out)
            def _():
                probs_copy(c).wait_recv()
                dv_acc[...] += grad_values_of(p_recv, c, lambda b: c_vm[:, cut(c * PACK + b)])

        for q in range(nseq):
            dv_t[q, g] = dv_acc[q * share : (q + 1) * share].astype(BF16)
        spread(lambda to: dv_t.at[to, g], lambda d: dv_r.at[d, g], 1, down, 0)

    def key_step(g):
        dk = None
        done = []
        for a in range(lots):
            c = g * lots + a

            @pl.when((c >= RAW) | whole_in)
            def _():
                dprobs_copy(c).wait_recv()

            ds_list = []
            for b in range(PACK):
                p = p_f32[c, lines(b), :]
                dp = dp_recv[c, lines(b), :].astype(F32)
                delta = jnp.sum(p * dp, axis=0, keepdims=True)
                ds = (p * (dp - delta)).astype(BF16)
                ds_list.append(ds)
                t = nn(ds, q_vm[:, cut(c * PACK + b)])
                dk = t if dk is None else dk + t
            done.append((c, jnp.concatenate(ds_list, axis=0)))
        dk = dk * scale
        for q in range(nseq):
            dk_t[q, g] = dk[q * share : (q + 1) * share]
        spread(lambda to: dk_t.at[to, g], lambda d: dk_r.at[d, g], 0, sec, 1)
        for c, ds in done:
            gq_vm[0, :, cut(c, wide)] = (tn(ds, k_bd[g]) * scale).astype(BF16)

    @pl.loop(0, 2 * groups)
    def _(i):
        early_v = jnp.where(sec == 0, START, jnp.where(sec == 1, groups, LATER))
        values_now = (i < early_v) | (i >= early_v + groups)
        g = jnp.where(i < early_v, i, jnp.where(values_now, i - groups, i - early_v))

        @pl.when(values_now)
        def _():
            value_step(g)

        @pl.when(jnp.logical_not(values_now))
        def _():
            key_step(g)

    def whole(src, dst, which):
        return remote(src, dst, sum_ss.at[which], sum_rs.at[which], same())

    dk_all = whole(dk_t.at[1:], dk_r.at[1:], 0)
    dv_all = whole(dv_t, dv_r, 1)
    rv_all = whole(rv_t.at[1:], rv_r.at[1:], 2)

    @pl.when(raw_in)
    def _():
        rv_all.wait_recv()

    dk_all.wait_recv()
    dv_all.wait_recv()
    for g in range(groups):
        dk = dk_t[seq, g]
        for d in range(1, nseq):
            dk = dk + dk_r[d, g]
        dv = dv_r[0, g].astype(F32)
        for d in range(1, nseq):
            dv = dv + dv_r[d, g].astype(F32)
        for c in range(RAW):
            if c // lots == g:
                dv = dv + rv_t[seq, c]
                for d in range(1, nseq):
                    dv = dv + rv_r[d, c]
        gk_out[0, :, g * D : (g + 1) * D] = dk.astype(BF16)
        gv_out[0, :, g * D : (g + 1) * D] = dv.astype(BF16)

    gathered(0, n - 1).wait_send()
    gathered(1, n - 1).wait_send()
    gathered(2, n).wait_send()
    dk_all.wait_send()
    dv_all.wait_send()

    def sent(ref, ss, everything):
        for first, where in ((0, everything), (RAW, jnp.logical_not(everything))):

            @pl.when(where)
            def _():
                part = ref.at[first:]
                remote(part, part, ss, raw_sem.at[1], same()).wait_send()

    sent(p_send, p_ss, whole_in)
    sent(dp_send, dp_ss, whole_out)

    @pl.when(raw_out)
    def _():
        raw.wait_send()

    @pl.when(raw_in)
    def _():
        rv_all.wait_send()


def put_out(*refs):
    sems = refs[8]
    copies = []
    for i in range(4):
        step = refs[i].shape[1] // CUTS if i < 2 else refs[i].shape[1]
        for j in range(refs[i].shape[1] // step):
            at = slice(j * step, (j + 1) * step)
            copies.append(
                pltpu.make_async_copy(refs[i].at[:, at], refs[4 + i].at[:, at], sems.at[i, j])
            )
    for c in copies:
        c.start()
    for c in copies:
        c.wait()


def per_device(nsec, nseq, ntp, queries, keys, values, cotangent, pattern, tile_owner):
    n = nseq * ntp
    part = keys.shape[1]
    width = keys.shape[2] // ntp
    rows = part * n
    groups = width // HEAD_SIZE
    text, cols = queries.shape[1:]
    share = rows // nseq
    nch = groups * (FAN // PACK)
    D = HEAD_SIZE
    dma = pltpu.SemaphoreType.DMA
    vm = pltpu.VMEM
    anyspace = pl.BlockSpec(memory_space=pl.ANY)
    smem = pl.BlockSpec(memory_space=pltpu.SMEM)
    vmem = pl.BlockSpec(memory_space=pltpu.VMEM)
    results = pl.pallas_call(
        functools.partial(kernel, nsec, nseq, ntp),
        out_shape=(
            vm((1, text, cols), BF16),
            vm((1, text, cols), BF16),
            vm((1, share, width), BF16),
            vm((1, share, width), BF16),
        ),
        in_specs=[anyspace] * 4 + [smem] * 2,
        out_specs=(vmem,) * 4,
        scratch_shapes=[
            vm((text, cols), BF16),
            vm((text, cols), BF16),
            vm((text, RAW * PACK * D), BF16),
            vm((3, n, part, width), BF16),
            vm((3, rows, width), F32),
            vm((3, rows, width), BF16),
            vm((groups, PACK * rows, PACK * D), BF16),
            vm((groups, PACK * rows, PACK * D), BF16),
            vm((nch, PACK * rows, text), F32),
            vm((nch, PACK * rows, text), BF16),
            vm((nch, PACK * rows, text), BF16),
            vm((nch, PACK * rows, text), BF16),
            vm((nch, PACK * rows, text), BF16),
            vm((nseq, groups, share, D), F32),
            vm((nseq, groups, share, D), F32),
            vm((rows, D), F32),
            vm((nseq, groups, share, D), BF16),
            vm((nseq, groups, share, D), BF16),
            vm((nseq, RAW, share, D), F32),
            vm((nseq, RAW, share, D), F32),
            dma((2,)), dma((2,)), dma((3,)), dma((3,)), dma((2,)),
            dma, dma((nch,)), dma, dma((nch,)), dma((3,)), dma((3,)),
            pltpu.SemaphoreType.REGULAR, pltpu.SemaphoreType.REGULAR,
        ],
        compiler_params=pltpu.CompilerParams(collective_id=0, has_side_effects=True),
        name="cross",
    )(queries, keys, values, cotangent, pattern, tile_owner)
    return pl.pallas_call(
        put_out,
        out_shape=tuple(jax.ShapeDtypeStruct(r.shape, r.dtype) for r in results),
        in_specs=[vmem] * 4,
        out_specs=(anyspace,) * 4,
        scratch_shapes=[dma((4, CUTS))],
        name="put",
    )(*[pltpu.with_memory_space_constraint(r, pltpu.VMEM) for r in results])


def solution(mesh):
    nsec, nseq, ntp = (mesh.shape[a] for a in ("section", "seq", "tp"))
    in_specs = (
        P("section", "seq", "tp"),
        P("section", ("seq", "tp"), None),
        P("section", ("seq", "tp"), None),
        P("section", "seq", "tp"),
        P("section", "seq", None),
        P("section", None),
    )
    out_specs = (P("section", "seq", "tp"),) * 4
    return jax.shard_map(
        functools.partial(per_device, nsec, nseq, ntp),
        mesh=mesh, in_specs=in_specs, out_specs=out_specs, check_vma=False,
    )
```

```python
import functools

import jax
import jax.numpy as jnp
from jax import lax
from jax.experimental import pallas as pl
from jax.experimental.pallas import tpu as pltpu
from jax.sharding import PartitionSpec as P

QUERY_HEADS = 64
KEY_VALUE_HEADS = 8
HEAD_SIZE = 128
FAN = QUERY_HEADS // KEY_VALUE_HEADS
PACK = 4
CUTS = 4
RAW = 1
AHEAD = 2
SPLIT = 3
HOLD = 2
START = 0
MESH = pl.DeviceIdType.MESH
F32 = jnp.float32
BF16 = jnp.bfloat16


def nt(a, b):
    return lax.dot_general(a, b, (((1,), (1,)), ((), ())), preferred_element_type=F32)


def nn(a, b):
    return lax.dot_general(a, b, (((1,), (0,)), ((), ())), preferred_element_type=F32)


def tn(a, b):
    return lax.dot_general(a, b, (((0,), (0,)), ((), ())), preferred_element_type=F32)


def cut(j, size=HEAD_SIZE):
    return pl.ds(pl.multiple_of(j * size, size), size)


def kernel(
    nsec, nseq, ntp,
    q_hbm, k_hbm, v_hbm, c_hbm, pat, own,
    att_vm, gq_vm, gk_out, gv_out,
    q_vm, c_vm, raw_vm,
    gath, asm, kvs,
    k_bd, v_bd,
    p_f32, p_send, p_recv, dp_send, dp_recv,
    dk_t, dk_r, dv_acc, dv_t, dv_r, dv_near, dv_out, dv_in, rv_t, rv_r,
    load_sem, own_sem, kv_ss, kv_rs, raw_sem,
    p_ss, p_rs, dp_ss, dp_rs, sum_ss, sum_rs,
    ready_up, ready_down,
):
    scale = HEAD_SIZE ** (-0.5)
    D = HEAD_SIZE
    n = nseq * ntp
    text, cols = q_vm.shape
    part = k_hbm.shape[1]
    width = k_hbm.shape[2] // ntp
    rows = part * n
    groups = width // D
    share = rows // nseq
    lots = FAN // PACK
    lot = PACK * rows
    wide = PACK * D
    nch = groups * lots
    sec, seq, tp = lax.axis_index("section"), lax.axis_index("seq"), lax.axis_index("tp")
    me = seq * ntp + tp
    up, down = lax.rem(sec + 1, nsec), lax.rem(sec + nsec - 1, nsec)
    last = nsec - 1
    inner = (sec > 0) & (sec < last)
    raw_in, raw_out = sec >= 0, sec >= 0
    whole_in, whole_out = jnp.logical_not(raw_in), jnp.logical_not(raw_out)

    def dev(s, i):
        return {"section": s, "seq": lax.div(i, ntp), "tp": lax.rem(i, ntp)}

    def signal(sem, to):
        pl.semaphore_signal(sem, inc=1, device_id=to, device_id_type=MESH)

    def remote(src, dst, ss, rs, to):
        return pltpu.make_async_remote_copy(
            src_ref=src, dst_ref=dst, send_sem=ss, recv_sem=rs, device_id=to, device_id_type=MESH
        )

    def same(s=sec):
        return {"section": s, "seq": seq, "tp": tp}

    barrier = pltpu.get_barrier_semaphore()

    @pl.loop(1, n)
    def _(d):
        signal(barrier, dev(sec, lax.rem(me + n - d, n)))

    @pl.when(sec < last)
    def _():
        signal(barrier, same(up))

    @pl.when(sec == 0)
    def _():
        @pl.loop(0, n)
        def _(d):
            signal(barrier, dev(down, lax.rem(me + d, n)))

    def half(ref, i):
        return ref.at[0, :, cut(lax.rem(i, ntp), width)]

    mine = [
        pltpu.make_async_copy(half(k_hbm, me), gath.at[0, me], own_sem.at[0]),
        pltpu.make_async_copy(half(v_hbm, me), gath.at[1, me], own_sem.at[1]),
    ]
    loads = [
        pltpu.make_async_copy(q_hbm.at[0], q_vm, load_sem.at[0]),
        pltpu.make_async_copy(c_hbm.at[0], c_vm, load_sem.at[1]),
    ]
    for c in mine + loads:
        c.start()

    from_others = jnp.where(sec > 0, 1, 0) + jnp.where(sec == last, n, 0)
    pl.semaphore_wait(barrier, n - 1 + from_others)

    @pl.when(sec > 0)
    def _():
        signal(ready_up, same(down))

    @pl.when(sec == last)
    def _():
        signal(ready_down, same(up))

    def gather(which, ref, to, d):
        peer = lax.rem(me + n - d, n)
        return remote(
            half(ref, peer), gath.at[which, me], kv_ss.at[which], kv_rs.at[which], dev(to, peer)
        )

    def gathered(which, count):
        return remote(
            gath.at[which, 0:count], gath.at[which, 0:count],
            kv_ss.at[which], kv_rs.at[which], same(),
        )

    @pl.loop(1, n)
    def _(d):
        gather(0, k_hbm, sec, d).start()

    raw = remote(
        c_hbm.at[0, :, 0 : RAW * wide], raw_vm, raw_sem.at[0], raw_sem.at[1], same(down)
    )

    @pl.when(inner & raw_out)
    def _():
        raw.start()

    @pl.when(sec < last)
    def _():
        pl.semaphore_wait(ready_up, 1)

    @pl.loop(0, n)
    def _(d):
        gather(2, v_hbm, up, d).start()

    @pl.when((sec == last) & raw_out)
    def _():
        raw.start()

    @pl.loop(1, n)
    def _(d):
        gather(1, v_hbm, sec, d).start()

    row_tile = lax.broadcasted_iota(jnp.int32, (rows, text), 0) // (rows // own.shape[1])
    blocks = pat.shape[1]
    lane_block = lax.broadcasted_iota(jnp.int32, (rows, text), 1) // (text // blocks)
    allowed = jnp.zeros((rows, text), jnp.bool_)
    for b in range(blocks):
        for t in range(own.shape[1]):
            owner = jnp.where(pat[0, b, t] > 0, own[0, t], -1)
            hit = row_tile == owner
            if blocks > 1:
                hit = hit & (lane_block == b)
            allowed = allowed | hit
    k_bd[...] = jnp.zeros_like(k_bd)
    v_bd[...] = jnp.zeros_like(v_bd)

    def assemble(which):
        for i in range(n):
            asm[which, part * i : part * (i + 1), :] = gath[which, i].astype(F32)
        kvs[which] = asm[which].astype(BF16)

    def lines(b):
        return slice(b * rows, (b + 1) * rows)

    def probs_copy(c):
        return remote(p_send.at[c], p_recv.at[c], p_ss, p_rs.at[c], same(up))

    def dprobs_copy(c):
        return remote(dp_send.at[c], dp_recv.at[c], dp_ss, dp_rs.at[c], same(down))

    def probs_of(c):
        key = kvs[0, :, cut(lax.div(c, lots))]
        for b in range(PACK):
            s = nt(key, q_vm[:, cut(c * PACK + b)]) * scale
            s = jnp.where(allowed, s, -jnp.inf)
            e = jnp.exp(s - jnp.max(s, axis=0, keepdims=True))
            p = e * (1.0 / jnp.sum(e, axis=0, keepdims=True))
            p_f32[c, lines(b), :] = p
            p_send[c, lines(b), :] = p.astype(BF16)

        @pl.when((c >= RAW) | whole_in)
        def _():
            probs_copy(c).start()

    def centred(value, block):
        dp = nt(value, block)
        return (dp - jnp.sum(dp, axis=0, keepdims=True) * (1.0 / rows)).astype(BF16)

    def dprobs_of(c):
        value = kvs[2, :, cut(lax.div(c, lots))]
        for b in range(PACK):
            dp_send[c, lines(b), :] = centred(value, c_vm[:, cut(c * PACK + b)])
        dprobs_copy(c).start()

    mine[0].wait()
    gathered(0, n - 1).wait_recv()
    assemble(0)
    loads[0].wait()

    @pl.when(sec == 0)
    def _():
        pl.semaphore_wait(ready_down, 1)
        raw.start()

    ahead = jnp.where(sec == 0, nch, jnp.where(sec == last, RAW + SPLIT, RAW + AHEAD))

    @pl.loop(0, ahead)
    def _(c):
        probs_of(c)

    mine[1].wait()
    gathered(1, n - 1).wait_recv()
    assemble(1)
    loads[1].wait()

    def attend():
        @pl.loop(0, groups)
        def _(g):
            key, value = kvs[0, :, cut(g)], kvs[1, :, cut(g)]
            for b in range(PACK):
                k_bd[g, lines(b), b * D : (b + 1) * D] = key
                v_bd[g, lines(b), b * D : (b + 1) * D] = value
            for a in range(lots):
                c = g * lots + a
                att_vm[0, :, cut(c, wide)] = tn(p_send[c], v_bd[g]).astype(BF16)

    @pl.when(sec == 0)
    def _():
        attend()

    gathered(2, n).wait_recv()
    assemble(2)

    lowest = jnp.where(whole_out, 0, RAW)

    @pl.loop(lowest, jnp.where(sec == last, nch + nch - ahead, nch))
    def _(i):
        @pl.when(i < nch)
        def _():
            dprobs_of(i)

        c = jnp.where(sec == last, i - nch, i - lowest) + ahead

        @pl.when((inner & (c < nch)) | (i >= nch))
        def _():
            probs_of(c)

    @pl.when(sec > 0)
    def _():
        attend()

    def grad_values_of(probs, c, block):
        dv = None
        for b in range(PACK):
            t = nn(probs[c, lines(b), :], block(b))
            dv = t if dv is None else dv + t
        return dv

    def spread(src, dst, which, to_sec, first):
        for d in range(first, nseq):
            to = lax.rem(seq + d, nseq)
            remote(
                src(to), dst(d), sum_ss.at[which], sum_rs.at[which],
                {"section": to_sec, "seq": to, "tp": tp},
            ).start()

    @pl.when(raw_in)
    def _():
        raw.wait_recv()
        for c in range(RAW):
            value = kvs[1, :, cut(c // lots)]

            def block(b):
                j = c * PACK + b
                return raw_vm[:, j * D : (j + 1) * D]

            for b in range(PACK):
                dp_recv[c, lines(b), :] = centred(value, block(b))
            dv = grad_values_of(p_send, c, block)
            for q in range(nseq):
                rv_t[q, c] = dv[q * share : (q + 1) * share]
        spread(lambda to: rv_t.at[to], lambda d: rv_r.at[d], 2, sec, 1)

    @pl.when(whole_in)
    def _():
        rv_t[...] = jnp.zeros_like(rv_t)
        rv_r[...] = jnp.zeros_like(rv_r)

    def whole(src, dst, which):
        return remote(src, dst, sum_ss.at[which], sum_rs.at[which], same())

    def value_step(g):
        dv_acc[...] = jnp.zeros_like(dv_acc)
        for a in range(lots):
            c = g * lots + a

            @pl.when((c >= RAW) | whole_out)
            def _():
                probs_copy(c).wait_recv()
                dv_acc[...] += grad_values_of(p_recv, c, lambda b: c_vm[:, cut(c * PACK + b)])

        for q in range(nseq):
            dv_t[q, g] = dv_acc[q * share : (q + 1) * share].astype(BF16)

        @pl.when(sec == 0)
        def _():
            spread(lambda to: dv_t.at[to, g], lambda d: dv_r.at[d, g], 1, down, 0)

        @pl.when(sec > 0)
        def _():
            spread(lambda to: dv_t.at[to, g], lambda d: dv_near.at[d, g], 3, sec, 1)

    def pass_values():
        whole(dv_t.at[1:], dv_near.at[1:], 3).wait_recv()
        for g in range(groups):
            dv = dv_t[seq, g].astype(F32)
            for d in range(1, nseq):
                dv = dv + dv_near[d, g].astype(F32)
            dv_out[g] = dv
        remote(dv_out, dv_in, sum_ss.at[4], sum_rs.at[4], same(down)).start()

    def key_step(g):
        dk = None
        done = []
        for a in range(lots):
            c = g * lots + a

            @pl.when((c >= RAW) | whole_in)
            def _():
                dprobs_copy(c).wait_recv()

            ds_list = []
            for b in range(PACK):
                p = p_f32[c, lines(b), :]
                dp = dp_recv[c, lines(b), :].astype(F32)
                delta = jnp.sum(p * dp, axis=0, keepdims=True)
                ds = (p * (dp - delta)).astype(BF16)
                ds_list.append(ds)
                t = nn(ds, q_vm[:, cut(c * PACK + b)])
                dk = t if dk is None else dk + t
            done.append((c, jnp.concatenate(ds_list, axis=0)))
        dk = dk * scale
        for q in range(nseq):
            dk_t[q, g] = dk[q * share : (q + 1) * share]
        spread(lambda to: dk_t.at[to, g], lambda d: dk_r.at[d, g], 0, sec, 1)
        for c, ds in done:
            gq_vm[0, :, cut(c, wide)] = (tn(ds, k_bd[g]) * scale).astype(BF16)

    @pl.loop(0, 2 * groups)
    def _(i):
        early_v = jnp.where(sec == 0, START, groups)
        values_now = (i < early_v) | (i >= early_v + groups)
        g = jnp.where(i < early_v, i, jnp.where(values_now, i - groups, i - early_v))

        @pl.when((sec > 0) & (i == groups + min(HOLD, groups - 1)))
        def _():
            pass_values()

        @pl.when(values_now)
        def _():
            value_step(g)

        @pl.when(jnp.logical_not(values_now))
        def _():
            key_step(g)

    dk_all = whole(dk_t.at[1:], dk_r.at[1:], 0)
    dv_all = whole(dv_t, dv_r, 1)
    rv_all = whole(rv_t.at[1:], rv_r.at[1:], 2)

    @pl.when(raw_in)
    def _():
        rv_all.wait_recv()

    dk_all.wait_recv()
    dv_pass = whole(dv_out, dv_in, 4)

    @pl.when(sec == last)
    def _():
        dv_all.wait_recv()
        for g in range(groups):
            dv = dv_r[0, g].astype(F32)
            for d in range(1, nseq):
                dv = dv + dv_r[d, g].astype(F32)
            dv_in[g] = dv

    @pl.when(sec < last)
    def _():
        dv_pass.wait_recv()

    for g in range(groups):
        dk = dk_t[seq, g]
        for d in range(1, nseq):
            dk = dk + dk_r[d, g]
        dv = dv_in[g]
        for c in range(RAW):
            if c // lots == g:
                dv = dv + rv_t[seq, c]
                for d in range(1, nseq):
                    dv = dv + rv_r[d, c]
        gk_out[0, :, g * D : (g + 1) * D] = dk.astype(BF16)
        gv_out[0, :, g * D : (g + 1) * D] = dv.astype(BF16)

    gathered(0, n - 1).wait_send()
    gathered(1, n - 1).wait_send()
    gathered(2, n).wait_send()
    dk_all.wait_send()

    @pl.when(sec == 0)
    def _():
        dv_all.wait_send()

    @pl.when(sec > 0)
    def _():
        whole(dv_t.at[1:], dv_near.at[1:], 3).wait_send()
        dv_pass.wait_send()


    def sent(ref, ss, everything):
        for first, where in ((0, everything), (RAW, jnp.logical_not(everything))):

            @pl.when(where)
            def _():
                part = ref.at[first:]
                remote(part, part, ss, raw_sem.at[1], same()).wait_send()

    sent(p_send, p_ss, whole_in)
    sent(dp_send, dp_ss, whole_out)

    @pl.when(raw_out)
    def _():
        raw.wait_send()

    @pl.when(raw_in)
    def _():
        rv_all.wait_send()


def put_out(*refs):
    sems = refs[8]
    copies = []
    for i in range(4):
        step = refs[i].shape[1] // CUTS if i < 2 else refs[i].shape[1]
        for j in range(refs[i].shape[1] // step):
            at = slice(j * step, (j + 1) * step)
            copies.append(
                pltpu.make_async_copy(refs[i].at[:, at], refs[4 + i].at[:, at], sems.at[i, j])
            )
    for c in copies:
        c.start()
    for c in copies:
        c.wait()


def per_device(nsec, nseq, ntp, queries, keys, values, cotangent, pattern, tile_owner):
    n = nseq * ntp
    part = keys.shape[1]
    width = keys.shape[2] // ntp
    rows = part * n
    groups = width // HEAD_SIZE
    text, cols = queries.shape[1:]
    share = rows // nseq
    nch = groups * (FAN // PACK)
    D = HEAD_SIZE
    dma = pltpu.SemaphoreType.DMA
    vm = pltpu.VMEM
    anyspace = pl.BlockSpec(memory_space=pl.ANY)
    smem = pl.BlockSpec(memory_space=pltpu.SMEM)
    vmem = pl.BlockSpec(memory_space=pltpu.VMEM)
    results = pl.pallas_call(
        functools.partial(kernel, nsec, nseq, ntp),
        out_shape=(
            vm((1, text, cols), BF16),
            vm((1, text, cols), BF16),
            vm((1, share, width), BF16),
            vm((1, share, width), BF16),
        ),
        in_specs=[anyspace] * 4 + [smem] * 2,
        out_specs=(vmem,) * 4,
        scratch_shapes=[
            vm((text, cols), BF16),
            vm((text, cols), BF16),
            vm((text, RAW * PACK * D), BF16),
            vm((3, n, part, width), BF16),
            vm((3, rows, width), F32),
            vm((3, rows, width), BF16),
            vm((groups, PACK * rows, PACK * D), BF16),
            vm((groups, PACK * rows, PACK * D), BF16),
            vm((nch, PACK * rows, text), F32),
            vm((nch, PACK * rows, text), BF16),
            vm((nch, PACK * rows, text), BF16),
            vm((nch, PACK * rows, text), BF16),
            vm((nch, PACK * rows, text), BF16),
            vm((nseq, groups, share, D), F32),
            vm((nseq, groups, share, D), F32),
            vm((rows, D), F32),
            vm((nseq, groups, share, D), BF16),
            vm((nseq, groups, share, D), BF16),
            vm((nseq, groups, share, D), BF16),
            vm((groups, share, D), F32),
            vm((groups, share, D), F32),
            vm((nseq, RAW, share, D), F32),
            vm((nseq, RAW, share, D), F32),
            dma((2,)), dma((2,)), dma((3,)), dma((3,)), dma((2,)),
            dma, dma((nch,)), dma, dma((nch,)), dma((5,)), dma((5,)),
            pltpu.SemaphoreType.REGULAR, pltpu.SemaphoreType.REGULAR,
        ],
        compiler_params=pltpu.CompilerParams(collective_id=0, has_side_effects=True),
        name="cross",
    )(queries, keys, values, cotangent, pattern, tile_owner)
    return pl.pallas_call(
        put_out,
        out_shape=tuple(jax.ShapeDtypeStruct(r.shape, r.dtype) for r in results),
        in_specs=[vmem] * 4,
        out_specs=(anyspace,) * 4,
        scratch_shapes=[dma((4, CUTS))],
        name="put",
    )(*[pltpu.with_memory_space_constraint(r, pltpu.VMEM) for r in results])


def solution(mesh):
    nsec, nseq, ntp = (mesh.shape[a] for a in ("section", "seq", "tp"))
    in_specs = (
        P("section", "seq", "tp"),
        P("section", ("seq", "tp"), None),
        P("section", ("seq", "tp"), None),
        P("section", "seq", "tp"),
        P("section", "seq", None),
        P("section", None),
    )
    out_specs = (P("section", "seq", "tp"),) * 4
    return jax.shard_map(
        functools.partial(per_device, nsec, nseq, ntp),
        mesh=mesh, in_specs=in_specs, out_specs=out_specs, check_vma=False,
    )
```

```python
import functools

import jax
import jax.numpy as jnp
from jax import lax
from jax.experimental import pallas as pl
from jax.experimental.pallas import tpu as pltpu
from jax.sharding import PartitionSpec as P

QUERY_HEADS = 64
KEY_VALUE_HEADS = 8
HEAD_SIZE = 128
FAN = QUERY_HEADS // KEY_VALUE_HEADS
PACK = 4
CUTS = 4
RAW = 1
AHEAD = 2
SPLIT = 3
HOLD = 2
START = 0
MESH = pl.DeviceIdType.MESH
F32 = jnp.float32
BF16 = jnp.bfloat16


def nt(a, b):
    return lax.dot_general(a, b, (((1,), (1,)), ((), ())), preferred_element_type=F32)


def nn(a, b):
    return lax.dot_general(a, b, (((1,), (0,)), ((), ())), preferred_element_type=F32)


def tn(a, b):
    return lax.dot_general(a, b, (((0,), (0,)), ((), ())), preferred_element_type=F32)


def cut(j, size=HEAD_SIZE):
    return pl.ds(pl.multiple_of(j * size, size), size)


def kernel(
    nsec, nseq, ntp,
    q_hbm, k_hbm, v_hbm, c_hbm, pat, own,
    att_vm, gq_vm, gk_out, gv_out,
    q_vm, c_vm, raw_vm,
    gath, asm, kvs,
    k_bd, v_bd,
    p_f32, p_send, p_recv, dp_send, dp_recv,
    dk_t, dk_r, dv_acc, dv_t, dv_r, dv_near, dv_out, dv_in, rv_t, rv_r,
    load_sem, own_sem, kv_ss, kv_rs, raw_sem,
    p_ss, p_rs, dp_ss, dp_rs, sum_ss, sum_rs,
    ready_up, ready_down,
):
    scale = HEAD_SIZE ** (-0.5)
    D = HEAD_SIZE
    n = nseq * ntp
    text, cols = q_vm.shape
    part = k_hbm.shape[1]
    width = k_hbm.shape[2] // ntp
    rows = part * n
    groups = width // D
    share = rows // nseq
    lots = FAN // PACK
    lot = PACK * rows
    wide = PACK * D
    nch = groups * lots
    sec, seq, tp = lax.axis_index("section"), lax.axis_index("seq"), lax.axis_index("tp")
    me = seq * ntp + tp
    up, down = lax.rem(sec + 1, nsec), lax.rem(sec + nsec - 1, nsec)
    last = nsec - 1
    inner = (sec > 0) & (sec < last)
    raw_in, raw_out = sec >= 0, sec >= 0
    whole_in, whole_out = jnp.logical_not(raw_in), jnp.logical_not(raw_out)

    def dev(s, i):
        return {"section": s, "seq": lax.div(i, ntp), "tp": lax.rem(i, ntp)}

    def signal(sem, to):
        pl.semaphore_signal(sem, inc=1, device_id=to, device_id_type=MESH)

    def remote(src, dst, ss, rs, to):
        return pltpu.make_async_remote_copy(
            src_ref=src, dst_ref=dst, send_sem=ss, recv_sem=rs, device_id=to, device_id_type=MESH
        )

    def same(s=sec):
        return {"section": s, "seq": seq, "tp": tp}

    barrier = pltpu.get_barrier_semaphore()

    for d in range(1, n):
        signal(barrier, dev(sec, lax.rem(me + n - d, n)))

    @pl.when(sec < last)
    def _():
        signal(barrier, same(up))

    @pl.when(sec == 0)
    def _():
        @pl.loop(0, n)
        def _(d):
            signal(barrier, dev(down, lax.rem(me + d, n)))

    def half(ref, i):
        return ref.at[0, :, cut(lax.rem(i, ntp), width)]

    mine = [
        pltpu.make_async_copy(half(k_hbm, me), gath.at[0, me], own_sem.at[0]),
        pltpu.make_async_copy(half(v_hbm, me), gath.at[1, me], own_sem.at[1]),
    ]
    loads = [
        pltpu.make_async_copy(q_hbm.at[0], q_vm, load_sem.at[0]),
        pltpu.make_async_copy(c_hbm.at[0], c_vm, load_sem.at[1]),
    ]
    for c in mine + loads:
        c.start()

    from_others = jnp.where(sec > 0, 1, 0) + jnp.where(sec == last, n, 0)
    pl.semaphore_wait(barrier, n - 1 + from_others)

    @pl.when(sec > 0)
    def _():
        signal(ready_up, same(down))

    @pl.when(sec == last)
    def _():
        signal(ready_down, same(up))

    def gather(which, ref, to, d):
        peer = lax.rem(me + n - d, n)
        return remote(
            half(ref, peer), gath.at[which, me], kv_ss.at[which], kv_rs.at[which], dev(to, peer)
        )

    def gathered(which, count):
        return remote(
            gath.at[which, 0:count], gath.at[which, 0:count],
            kv_ss.at[which], kv_rs.at[which], same(),
        )

    for d in range(1, n):
        gather(0, k_hbm, sec, d).start()

    raw = remote(
        c_hbm.at[0, :, 0 : RAW * wide], raw_vm, raw_sem.at[0], raw_sem.at[1], same(down)
    )

    @pl.when(inner & raw_out)
    def _():
        raw.start()

    @pl.when(sec < last)
    def _():
        pl.semaphore_wait(ready_up, 1)

    for d in range(n):
        gather(2, v_hbm, up, d).start()

    @pl.when((sec == last) & raw_out)
    def _():
        raw.start()

    @pl.loop(1, n)
    def _(d):
        gather(1, v_hbm, sec, d).start()

    row_tile = lax.broadcasted_iota(jnp.int32, (rows, text), 0) // (rows // own.shape[1])
    blocks = pat.shape[1]
    lane_block = lax.broadcasted_iota(jnp.int32, (rows, text), 1) // (text // blocks)
    allowed = jnp.zeros((rows, text), jnp.bool_)
    for b in range(blocks):
        for t in range(own.shape[1]):
            owner = jnp.where(pat[0, b, t] > 0, own[0, t], -1)
            hit = row_tile == owner
            if blocks > 1:
                hit = hit & (lane_block == b)
            allowed = allowed | hit
    k_bd[...] = jnp.zeros_like(k_bd)
    v_bd[...] = jnp.zeros_like(v_bd)

    def assemble(which):
        kvs[which] = jnp.concatenate([gath[which, i] for i in range(n)], axis=0)

    def lines(b):
        return slice(b * rows, (b + 1) * rows)

    def probs_copy(c):
        return remote(p_send.at[c], p_recv.at[c], p_ss, p_rs.at[c], same(up))

    def dprobs_copy(c):
        return remote(dp_send.at[c], dp_recv.at[c], dp_ss, dp_rs.at[c], same(down))

    def probs_of(c):
        key = kvs[0, :, cut(lax.div(c, lots))]
        for b in range(PACK):
            s = nt(key, q_vm[:, cut(c * PACK + b)]) * scale
            s = jnp.where(allowed, s, -jnp.inf)
            e = jnp.exp(s - jnp.max(s, axis=0, keepdims=True))
            p = e * (1.0 / jnp.sum(e, axis=0, keepdims=True))
            p_f32[c, lines(b), :] = p
            p_send[c, lines(b), :] = p.astype(BF16)

        @pl.when((c >= RAW) | whole_in)
        def _():
            probs_copy(c).start()

    def centred(value, block):
        dp = nt(value, block)
        return (dp - jnp.sum(dp, axis=0, keepdims=True) * (1.0 / rows)).astype(BF16)

    def dprobs_of(c):
        value = kvs[2, :, cut(lax.div(c, lots))]
        for b in range(PACK):
            dp_send[c, lines(b), :] = centred(value, c_vm[:, cut(c * PACK + b)])
        dprobs_copy(c).start()

    mine[0].wait()
    gathered(0, n - 1).wait_recv()
    assemble(0)
    loads[0].wait()

    @pl.when(sec == 0)
    def _():
        pl.semaphore_wait(ready_down, 1)
        raw.start()

    ahead = jnp.where(sec == 0, nch, jnp.where(sec == last, RAW + SPLIT, RAW + AHEAD))

    @pl.loop(0, ahead)
    def _(c):
        probs_of(c)

    mine[1].wait()
    gathered(1, n - 1).wait_recv()
    assemble(1)
    loads[1].wait()

    def attend():
        @pl.loop(0, groups)
        def _(g):
            key, value = kvs[0, :, cut(g)], kvs[1, :, cut(g)]
            for b in range(PACK):
                k_bd[g, lines(b), b * D : (b + 1) * D] = key
                v_bd[g, lines(b), b * D : (b + 1) * D] = value
            for a in range(lots):
                c = g * lots + a
                att_vm[0, :, cut(c, wide)] = tn(p_send[c], v_bd[g]).astype(BF16)

    @pl.when(sec == 0)
    def _():
        attend()

    gathered(2, n).wait_recv()
    assemble(2)

    lowest = jnp.where(whole_out, 0, RAW)

    @pl.loop(lowest, jnp.where(sec == last, nch + nch - ahead, nch))
    def _(i):
        @pl.when(i < nch)
        def _():
            dprobs_of(i)

        c = jnp.where(sec == last, i - nch, i - lowest) + ahead

        @pl.when((inner & (c < nch)) | (i >= nch))
        def _():
            probs_of(c)

    @pl.when(sec > 0)
    def _():
        attend()

    def grad_values_of(probs, c, block):
        dv = None
        for b in range(PACK):
            t = nn(probs[c, lines(b), :], block(b))
            dv = t if dv is None else dv + t
        return dv

    def spread(src, dst, which, to_sec, first):
        for d in range(first, nseq):
            to = lax.rem(seq + d, nseq)
            remote(
                src(to), dst(d), sum_ss.at[which], sum_rs.at[which],
                {"section": to_sec, "seq": to, "tp": tp},
            ).start()

    @pl.when(raw_in)
    def _():
        raw.wait_recv()
        for c in range(RAW):
            value = kvs[1, :, cut(c // lots)]

            def block(b):
                j = c * PACK + b
                return raw_vm[:, j * D : (j + 1) * D]

            for b in range(PACK):
                dp_recv[c, lines(b), :] = centred(value, block(b))
            dv = grad_values_of(p_send, c, block)
            for q in range(nseq):
                rv_t[q, c] = dv[q * share : (q + 1) * share]
        spread(lambda to: rv_t.at[to], lambda d: rv_r.at[d], 2, sec, 1)

    @pl.when(whole_in)
    def _():
        rv_t[...] = jnp.zeros_like(rv_t)
        rv_r[...] = jnp.zeros_like(rv_r)

    def whole(src, dst, which):
        return remote(src, dst, sum_ss.at[which], sum_rs.at[which], same())

    def value_step(g):
        dv_acc[...] = jnp.zeros_like(dv_acc)
        for a in range(lots):
            c = g * lots + a

            @pl.when((c >= RAW) | whole_out)
            def _():
                probs_copy(c).wait_recv()
                dv_acc[...] += grad_values_of(p_recv, c, lambda b: c_vm[:, cut(c * PACK + b)])

        for q in range(nseq):
            dv_t[q, g] = dv_acc[q * share : (q + 1) * share].astype(BF16)

        @pl.when(sec == 0)
        def _():
            spread(lambda to: dv_t.at[to, g], lambda d: dv_r.at[d, g], 1, down, 0)

        @pl.when(sec > 0)
        def _():
            spread(lambda to: dv_t.at[to, g], lambda d: dv_near.at[d, g], 3, sec, 1)

    def pass_values():
        whole(dv_t.at[1:], dv_near.at[1:], 3).wait_recv()
        for g in range(groups):
            dv = dv_t[seq, g].astype(F32)
            for d in range(1, nseq):
                dv = dv + dv_near[d, g].astype(F32)
            dv_out[g] = dv
        remote(dv_out, dv_in, sum_ss.at[4], sum_rs.at[4], same(down)).start()

    def key_step(g):
        dk = None
        done = []
        for a in range(lots):
            c = g * lots + a

            @pl.when((c >= RAW) | whole_in)
            def _():
                dprobs_copy(c).wait_recv()

            ds_list = []
            for b in range(PACK):
                p = p_f32[c, lines(b), :]
                dp = dp_recv[c, lines(b), :].astype(F32)
                delta = jnp.sum(p * dp, axis=0, keepdims=True)
                ds = (p * (dp - delta)).astype(BF16)
                ds_list.append(ds)
                t = nn(ds, q_vm[:, cut(c * PACK + b)])
                dk = t if dk is None else dk + t
            done.append((c, jnp.concatenate(ds_list, axis=0)))
        dk = dk * scale
        for q in range(nseq):
            dk_t[q, g] = dk[q * share : (q + 1) * share]
        spread(lambda to: dk_t.at[to, g], lambda d: dk_r.at[d, g], 0, sec, 1)
        for c, ds in done:
            gq_vm[0, :, cut(c, wide)] = (tn(ds, k_bd[g]) * scale).astype(BF16)

    @pl.loop(0, 2 * groups)
    def _(i):
        early_v = jnp.where(sec == 0, START, groups)
        values_now = (i < early_v) | (i >= early_v + groups)
        g = jnp.where(i < early_v, i, jnp.where(values_now, i - groups, i - early_v))

        @pl.when((sec > 0) & (i == groups + min(HOLD, groups - 1)))
        def _():
            pass_values()

        @pl.when(values_now)
        def _():
            value_step(g)

        @pl.when(jnp.logical_not(values_now))
        def _():
            key_step(g)

    dk_all = whole(dk_t.at[1:], dk_r.at[1:], 0)
    dv_all = whole(dv_t, dv_r, 1)
    rv_all = whole(rv_t.at[1:], rv_r.at[1:], 2)

    @pl.when(raw_in)
    def _():
        rv_all.wait_recv()

    dk_all.wait_recv()
    dv_pass = whole(dv_out, dv_in, 4)

    @pl.when(sec == last)
    def _():
        dv_all.wait_recv()
        for g in range(groups):
            dv = dv_r[0, g].astype(F32)
            for d in range(1, nseq):
                dv = dv + dv_r[d, g].astype(F32)
            dv_in[g] = dv

    @pl.when(sec < last)
    def _():
        dv_pass.wait_recv()

    for g in range(groups):
        dk = dk_t[seq, g]
        for d in range(1, nseq):
            dk = dk + dk_r[d, g]
        dv = dv_in[g]
        for c in range(RAW):
            if c // lots == g:
                dv = dv + rv_t[seq, c]
                for d in range(1, nseq):
                    dv = dv + rv_r[d, c]
        gk_out[0, :, g * D : (g + 1) * D] = dk.astype(BF16)
        gv_out[0, :, g * D : (g + 1) * D] = dv.astype(BF16)

    gathered(0, n - 1).wait_send()
    gathered(1, n - 1).wait_send()
    gathered(2, n).wait_send()
    dk_all.wait_send()

    @pl.when(sec == 0)
    def _():
        dv_all.wait_send()

    @pl.when(sec > 0)
    def _():
        whole(dv_t.at[1:], dv_near.at[1:], 3).wait_send()
        dv_pass.wait_send()


    def sent(ref, ss, everything):
        for first, where in ((0, everything), (RAW, jnp.logical_not(everything))):

            @pl.when(where)
            def _():
                part = ref.at[first:]
                remote(part, part, ss, raw_sem.at[1], same()).wait_send()

    sent(p_send, p_ss, whole_in)
    sent(dp_send, dp_ss, whole_out)

    @pl.when(raw_out)
    def _():
        raw.wait_send()

    @pl.when(raw_in)
    def _():
        rv_all.wait_send()


def put_out(*refs):
    sems = refs[8]
    copies = []
    for i in range(4):
        step = refs[i].shape[1] // CUTS if i < 2 else refs[i].shape[1]
        for j in range(refs[i].shape[1] // step):
            at = slice(j * step, (j + 1) * step)
            copies.append(
                pltpu.make_async_copy(refs[i].at[:, at], refs[4 + i].at[:, at], sems.at[i, j])
            )
    for c in copies:
        c.start()
    for c in copies:
        c.wait()


def per_device(nsec, nseq, ntp, queries, keys, values, cotangent, pattern, tile_owner):
    n = nseq * ntp
    part = keys.shape[1]
    width = keys.shape[2] // ntp
    rows = part * n
    groups = width // HEAD_SIZE
    text, cols = queries.shape[1:]
    share = rows // nseq
    nch = groups * (FAN // PACK)
    D = HEAD_SIZE
    dma = pltpu.SemaphoreType.DMA
    vm = pltpu.VMEM
    anyspace = pl.BlockSpec(memory_space=pl.ANY)
    smem = pl.BlockSpec(memory_space=pltpu.SMEM)
    vmem = pl.BlockSpec(memory_space=pltpu.VMEM)
    results = pl.pallas_call(
        functools.partial(kernel, nsec, nseq, ntp),
        out_shape=(
            vm((1, text, cols), BF16),
            vm((1, text, cols), BF16),
            vm((1, share, width), BF16),
            vm((1, share, width), BF16),
        ),
        in_specs=[anyspace] * 4 + [smem] * 2,
        out_specs=(vmem,) * 4,
        scratch_shapes=[
            vm((text, cols), BF16),
            vm((text, cols), BF16),
            vm((text, RAW * PACK * D), BF16),
            vm((3, n, part, width), BF16),
            vm((3, rows, width), F32),
            vm((3, rows, width), BF16),
            vm((groups, PACK * rows, PACK * D), BF16),
            vm((groups, PACK * rows, PACK * D), BF16),
            vm((nch, PACK * rows, text), F32),
            vm((nch, PACK * rows, text), BF16),
            vm((nch, PACK * rows, text), BF16),
            vm((nch, PACK * rows, text), BF16),
            vm((nch, PACK * rows, text), BF16),
            vm((nseq, groups, share, D), F32),
            vm((nseq, groups, share, D), F32),
            vm((rows, D), F32),
            vm((nseq, groups, share, D), BF16),
            vm((nseq, groups, share, D), BF16),
            vm((nseq, groups, share, D), BF16),
            vm((groups, share, D), F32),
            vm((groups, share, D), F32),
            vm((nseq, RAW, share, D), F32),
            vm((nseq, RAW, share, D), F32),
            dma((2,)), dma((2,)), dma((3,)), dma((3,)), dma((2,)),
            dma, dma((nch,)), dma, dma((nch,)), dma((5,)), dma((5,)),
            pltpu.SemaphoreType.REGULAR, pltpu.SemaphoreType.REGULAR,
        ],
        compiler_params=pltpu.CompilerParams(collective_id=0, has_side_effects=True),
        name="cross",
    )(queries, keys, values, cotangent, pattern, tile_owner)
    return pl.pallas_call(
        put_out,
        out_shape=tuple(jax.ShapeDtypeStruct(r.shape, r.dtype) for r in results),
        in_specs=[vmem] * 4,
        out_specs=(anyspace,) * 4,
        scratch_shapes=[dma((4, CUTS))],
        name="put",
    )(*[pltpu.with_memory_space_constraint(r, pltpu.VMEM) for r in results])


def solution(mesh):
    nsec, nseq, ntp = (mesh.shape[a] for a in ("section", "seq", "tp"))
    in_specs = (
        P("section", "seq", "tp"),
        P("section", ("seq", "tp"), None),
        P("section", ("seq", "tp"), None),
        P("section", "seq", "tp"),
        P("section", "seq", None),
        P("section", None),
    )
    out_specs = (P("section", "seq", "tp"),) * 4
    return jax.shard_map(
        functools.partial(per_device, nsec, nseq, ntp),
        mesh=mesh, in_specs=in_specs, out_specs=out_specs, check_vma=False,
    )
```

```python
import functools

import jax
import jax.numpy as jnp
from jax import lax
from jax.experimental import pallas as pl
from jax.experimental.pallas import tpu as pltpu
from jax.sharding import PartitionSpec as P

QUERY_HEADS = 64
KEY_VALUE_HEADS = 8
HEAD_SIZE = 128
FAN = QUERY_HEADS // KEY_VALUE_HEADS
PACK = 4
CUTS = 4
RAW = 1
AHEAD = 7
SPLIT = 3
HOLD = 2
START = 0
MESH = pl.DeviceIdType.MESH
F32 = jnp.float32
BF16 = jnp.bfloat16


def nt(a, b):
    return lax.dot_general(a, b, (((1,), (1,)), ((), ())), preferred_element_type=F32)


def nn(a, b):
    return lax.dot_general(a, b, (((1,), (0,)), ((), ())), preferred_element_type=F32)


def tn(a, b):
    return lax.dot_general(a, b, (((0,), (0,)), ((), ())), preferred_element_type=F32)


def cut(j, size=HEAD_SIZE):
    return pl.ds(pl.multiple_of(j * size, size), size)


def kernel(
    nsec, nseq, ntp,
    q_hbm, k_hbm, v_hbm, c_hbm, pat, own,
    att_vm, gq_vm, gk_out, gv_out,
    q_vm, c_vm, raw_vm,
    gath, asm, kvs,
    k_bd, v_bd,
    p_f32, p_send, p_recv, dp_send, dp_recv,
    dk_t, dk_r, dv_acc, dv_t, dv_r, dv_near, dv_out, dv_in, rv_t, rv_r,
    load_sem, own_sem, kv_ss, kv_rs, raw_sem,
    p_ss, p_rs, dp_ss, dp_rs, sum_ss, sum_rs,
    ready_up, ready_down,
):
    scale = HEAD_SIZE ** (-0.5)
    D = HEAD_SIZE
    n = nseq * ntp
    text, cols = q_vm.shape
    part = k_hbm.shape[1]
    width = k_hbm.shape[2] // ntp
    rows = part * n
    groups = width // D
    share = rows // nseq
    lots = FAN // PACK
    lot = PACK * rows
    wide = PACK * D
    nch = groups * lots
    sec, seq, tp = lax.axis_index("section"), lax.axis_index("seq"), lax.axis_index("tp")
    me = seq * ntp + tp
    up, down = lax.rem(sec + 1, nsec), lax.rem(sec + nsec - 1, nsec)
    last = nsec - 1
    inner = (sec > 0) & (sec < last)
    raw_in, raw_out = sec >= 0, sec >= 0
    whole_in, whole_out = jnp.logical_not(raw_in), jnp.logical_not(raw_out)

    def dev(s, i):
        return {"section": s, "seq": lax.div(i, ntp), "tp": lax.rem(i, ntp)}

    def signal(sem, to):
        pl.semaphore_signal(sem, inc=1, device_id=to, device_id_type=MESH)

    def remote(src, dst, ss, rs, to):
        return pltpu.make_async_remote_copy(
            src_ref=src, dst_ref=dst, send_sem=ss, recv_sem=rs, device_id=to, device_id_type=MESH
        )

    def same(s=sec):
        return {"section": s, "seq": seq, "tp": tp}

    barrier = pltpu.get_barrier_semaphore()

    @pl.loop(1, n)
    def _(d):
        signal(barrier, dev(sec, lax.rem(me + n - d, n)))

    @pl.when(sec < last)
    def _():
        signal(barrier, same(up))

    @pl.when(sec == 0)
    def _():
        @pl.loop(0, n)
        def _(d):
            signal(barrier, dev(down, lax.rem(me + d, n)))

    def half(ref, i):
        return ref.at[0, :, cut(lax.rem(i, ntp), width)]

    mine = [
        pltpu.make_async_copy(half(k_hbm, me), gath.at[0, me], own_sem.at[0]),
        pltpu.make_async_copy(half(v_hbm, me), gath.at[1, me], own_sem.at[1]),
    ]
    loads = [
        pltpu.make_async_copy(q_hbm.at[0], q_vm, load_sem.at[0]),
        pltpu.make_async_copy(c_hbm.at[0], c_vm, load_sem.at[1]),
    ]
    for c in mine + loads:
        c.start()

    from_others = jnp.where(sec > 0, 1, 0) + jnp.where(sec == last, n, 0)
    pl.semaphore_wait(barrier, n - 1 + from_others)

    @pl.when(sec > 0)
    def _():
        signal(ready_up, same(down))

    @pl.when(sec == last)
    def _():
        signal(ready_down, same(up))

    def gather(which, ref, to, d):
        peer = lax.rem(me + d, n)
        return remote(
            half(ref, peer), gath.at[which, me], kv_ss.at[which], kv_rs.at[which], dev(to, peer)
        )

    def gathered(which, count):
        return remote(
            gath.at[which, 0:count], gath.at[which, 0:count],
            kv_ss.at[which], kv_rs.at[which], same(),
        )

    @pl.loop(1, n)
    def _(d):
        gather(0, k_hbm, sec, d).start()

    raw = remote(
        c_hbm.at[0, :, 0 : RAW * wide], raw_vm, raw_sem.at[0], raw_sem.at[1], same(down)
    )

    @pl.when(inner & raw_out)
    def _():
        raw.start()

    @pl.when(sec < last)
    def _():
        pl.semaphore_wait(ready_up, 1)

    @pl.loop(0, n)
    def _(d):
        gather(2, v_hbm, up, d).start()

    @pl.when((sec == last) & raw_out)
    def _():
        raw.start()

    @pl.loop(1, n)
    def _(d):
        gather(1, v_hbm, sec, d).start()

    row_tile = lax.broadcasted_iota(jnp.int32, (rows, text), 0) // (rows // own.shape[1])
    blocks = pat.shape[1]
    lane_block = lax.broadcasted_iota(jnp.int32, (rows, text), 1) // (text // blocks)
    allowed = jnp.zeros((rows, text), jnp.bool_)
    for b in range(blocks):
        for t in range(own.shape[1]):
            owner = jnp.where(pat[0, b, t] > 0, own[0, t], -1)
            hit = row_tile == owner
            if blocks > 1:
                hit = hit & (lane_block == b)
            allowed = allowed | hit
    k_bd[...] = jnp.zeros_like(k_bd)
    v_bd[...] = jnp.zeros_like(v_bd)

    def assemble(which):
        for i in range(n):
            asm[which, part * i : part * (i + 1), :] = gath[which, i].astype(F32)
        kvs[which] = asm[which].astype(BF16)

    def lines(b):
        return slice(b * rows, (b + 1) * rows)

    def probs_copy(c):
        return remote(p_send.at[c], p_recv.at[c], p_ss, p_rs.at[c], same(up))

    def dprobs_copy(c):
        return remote(dp_send.at[c], dp_recv.at[c], dp_ss, dp_rs.at[c], same(down))

    def probs_of(c):
        key = kvs[0, :, cut(lax.div(c, lots))]
        for b in range(PACK):
            s = nt(key, q_vm[:, cut(c * PACK + b)]) * scale
            s = jnp.where(allowed, s, -jnp.inf)
            e = jnp.exp(s - jnp.max(s, axis=0, keepdims=True))
            p = e * (1.0 / jnp.sum(e, axis=0, keepdims=True))
            p_f32[c, lines(b), :] = p
            p_send[c, lines(b), :] = p.astype(BF16)

        @pl.when((c >= RAW) | whole_in)
        def _():
            probs_copy(c).start()

    def centred(value, block):
        dp = nt(value, block)
        return (dp - jnp.sum(dp, axis=0, keepdims=True) * (1.0 / rows)).astype(BF16)

    def dprobs_of(c):
        value = kvs[2, :, cut(lax.div(c, lots))]
        for b in range(PACK):
            dp_send[c, lines(b), :] = centred(value, c_vm[:, cut(c * PACK + b)])
        dprobs_copy(c).start()

    mine[0].wait()
    gathered(0, n - 1).wait_recv()
    assemble(0)
    loads[0].wait()

    @pl.when(sec == 0)
    def _():
        pl.semaphore_wait(ready_down, 1)
        raw.start()

    ahead = jnp.where(sec == 0, nch, jnp.where(sec == last, RAW + SPLIT, RAW + AHEAD))

    @pl.loop(0, ahead)
    def _(c):
        probs_of(c)

    mine[1].wait()
    gathered(1, n - 1).wait_recv()
    assemble(1)
    loads[1].wait()

    def attend():
        @pl.loop(0, groups)
        def _(g):
            key, value = kvs[0, :, cut(g)], kvs[1, :, cut(g)]
            for b in range(PACK):
                k_bd[g, lines(b), b * D : (b + 1) * D] = key
                v_bd[g, lines(b), b * D : (b + 1) * D] = value
            for a in range(lots):
                c = g * lots + a
                att_vm[0, :, cut(c, wide)] = tn(p_send[c], v_bd[g]).astype(BF16)

    @pl.when(sec == 0)
    def _():
        attend()

    gathered(2, n).wait_recv()
    assemble(2)

    lowest = jnp.where(whole_out, 0, RAW)

    @pl.loop(lowest, jnp.where(sec == last, nch + nch - ahead, nch))
    def _(i):
        @pl.when(i < nch)
        def _():
            dprobs_of(i)

        c = jnp.where(sec == last, i - nch, i - lowest) + ahead

        @pl.when((inner & (c < nch)) | (i >= nch))
        def _():
            probs_of(c)

    @pl.when(sec > 0)
    def _():
        attend()

    def grad_values_of(probs, c, block):
        dv = None
        for b in range(PACK):
            t = nn(probs[c, lines(b), :], block(b))
            dv = t if dv is None else dv + t
        return dv

    def spread(src, dst, which, to_sec, first):
        for d in range(first, nseq):
            to = lax.rem(seq + d, nseq)
            remote(
                src(to), dst(d), sum_ss.at[which], sum_rs.at[which],
                {"section": to_sec, "seq": to, "tp": tp},
            ).start()

    @pl.when(raw_in)
    def _():
        raw.wait_recv()
        for c in range(RAW):
            value = kvs[1, :, cut(c // lots)]

            def block(b):
                j = c * PACK + b
                return raw_vm[:, j * D : (j + 1) * D]

            for b in range(PACK):
                dp_recv[c, lines(b), :] = centred(value, block(b))
            dv = grad_values_of(p_send, c, block)
            for q in range(nseq):
                rv_t[q, c] = dv[q * share : (q + 1) * share]
        spread(lambda to: rv_t.at[to], lambda d: rv_r.at[d], 2, sec, 1)

    @pl.when(whole_in)
    def _():
        rv_t[...] = jnp.zeros_like(rv_t)
        rv_r[...] = jnp.zeros_like(rv_r)

    def whole(src, dst, which):
        return remote(src, dst, sum_ss.at[which], sum_rs.at[which], same())

    def value_step(g):
        dv_acc[...] = jnp.zeros_like(dv_acc)
        for a in range(lots):
            c = g * lots + a

            @pl.when((c >= RAW) | whole_out)
            def _():
                probs_copy(c).wait_recv()
                dv_acc[...] += grad_values_of(p_recv, c, lambda b: c_vm[:, cut(c * PACK + b)])

        for q in range(nseq):
            dv_t[q, g] = dv_acc[q * share : (q + 1) * share].astype(BF16)

        @pl.when(sec == 0)
        def _():
            spread(lambda to: dv_t.at[to, g], lambda d: dv_r.at[d, g], 1, down, 0)

        @pl.when(sec > 0)
        def _():
            spread(lambda to: dv_t.at[to, g], lambda d: dv_near.at[d, g], 3, sec, 1)

    def pass_values():
        whole(dv_t.at[1:], dv_near.at[1:], 3).wait_recv()
        for g in range(groups):
            dv = dv_t[seq, g].astype(F32)
            for d in range(1, nseq):
                dv = dv + dv_near[d, g].astype(F32)
            dv_out[g] = dv
        remote(dv_out, dv_in, sum_ss.at[4], sum_rs.at[4], same(down)).start()

    def key_step(g):
        dk = None
        done = []
        for a in range(lots):
            c = g * lots + a

            @pl.when((c >= RAW) | whole_in)
            def _():
                dprobs_copy(c).wait_recv()

            ds_list = []
            for b in range(PACK):
                p = p_f32[c, lines(b), :]
                dp = dp_recv[c, lines(b), :].astype(F32)
                delta = jnp.sum(p * dp, axis=0, keepdims=True)
                ds = (p * (dp - delta)).astype(BF16)
                ds_list.append(ds)
                t = nn(ds, q_vm[:, cut(c * PACK + b)])
                dk = t if dk is None else dk + t
            done.append((c, jnp.concatenate(ds_list, axis=0)))
        dk = dk * scale
        for q in range(nseq):
            dk_t[q, g] = dk[q * share : (q + 1) * share]
        spread(lambda to: dk_t.at[to, g], lambda d: dk_r.at[d, g], 0, sec, 1)
        for c, ds in done:
            gq_vm[0, :, cut(c, wide)] = (tn(ds, k_bd[g]) * scale).astype(BF16)

    @pl.loop(0, 2 * groups)
    def _(i):
        early_v = jnp.where(sec == 0, START, groups)
        values_now = (i < early_v) | (i >= early_v + groups)
        g = jnp.where(i < early_v, i, jnp.where(values_now, i - groups, i - early_v))

        @pl.when((sec > 0) & (i == groups + min(HOLD, groups - 1)))
        def _():
            pass_values()

        @pl.when(values_now)
        def _():
            value_step(g)

        @pl.when(jnp.logical_not(values_now))
        def _():
            key_step(g)

    dk_all = whole(dk_t.at[1:], dk_r.at[1:], 0)
    dv_all = whole(dv_t, dv_r, 1)
    rv_all = whole(rv_t.at[1:], rv_r.at[1:], 2)

    @pl.when(raw_in)
    def _():
        rv_all.wait_recv()

    dk_all.wait_recv()
    dv_pass = whole(dv_out, dv_in, 4)

    @pl.when(sec == last)
    def _():
        dv_all.wait_recv()
        for g in range(groups):
            dv = dv_r[0, g].astype(F32)
            for d in range(1, nseq):
                dv = dv + dv_r[d, g].astype(F32)
            dv_in[g] = dv

    @pl.when(sec < last)
    def _():
        dv_pass.wait_recv()

    for g in range(groups):
        dk = dk_t[seq, g]
        for d in range(1, nseq):
            dk = dk + dk_r[d, g]
        dv = dv_in[g]
        for c in range(RAW):
            if c // lots == g:
                dv = dv + rv_t[seq, c]
                for d in range(1, nseq):
                    dv = dv + rv_r[d, c]
        gk_out[0, :, g * D : (g + 1) * D] = dk.astype(BF16)
        gv_out[0, :, g * D : (g + 1) * D] = dv.astype(BF16)

    gathered(0, n - 1).wait_send()
    gathered(1, n - 1).wait_send()
    gathered(2, n).wait_send()
    dk_all.wait_send()

    @pl.when(sec == 0)
    def _():
        dv_all.wait_send()

    @pl.when(sec > 0)
    def _():
        whole(dv_t.at[1:], dv_near.at[1:], 3).wait_send()
        dv_pass.wait_send()


    def sent(ref, ss, everything):
        for first, where in ((0, everything), (RAW, jnp.logical_not(everything))):

            @pl.when(where)
            def _():
                part = ref.at[first:]
                remote(part, part, ss, raw_sem.at[1], same()).wait_send()

    sent(p_send, p_ss, whole_in)
    sent(dp_send, dp_ss, whole_out)

    @pl.when(raw_out)
    def _():
        raw.wait_send()

    @pl.when(raw_in)
    def _():
        rv_all.wait_send()


def put_out(*refs):
    sems = refs[8]
    copies = []
    for i in range(4):
        step = refs[i].shape[1] // CUTS if i < 2 else refs[i].shape[1]
        for j in range(refs[i].shape[1] // step):
            at = slice(j * step, (j + 1) * step)
            copies.append(
                pltpu.make_async_copy(refs[i].at[:, at], refs[4 + i].at[:, at], sems.at[i, j])
            )
    for c in copies:
        c.start()
    for c in copies:
        c.wait()


def per_device(nsec, nseq, ntp, queries, keys, values, cotangent, pattern, tile_owner):
    n = nseq * ntp
    part = keys.shape[1]
    width = keys.shape[2] // ntp
    rows = part * n
    groups = width // HEAD_SIZE
    text, cols = queries.shape[1:]
    share = rows // nseq
    nch = groups * (FAN // PACK)
    D = HEAD_SIZE
    dma = pltpu.SemaphoreType.DMA
    vm = pltpu.VMEM
    anyspace = pl.BlockSpec(memory_space=pl.ANY)
    smem = pl.BlockSpec(memory_space=pltpu.SMEM)
    vmem = pl.BlockSpec(memory_space=pltpu.VMEM)
    results = pl.pallas_call(
        functools.partial(kernel, nsec, nseq, ntp),
        out_shape=(
            vm((1, text, cols), BF16),
            vm((1, text, cols), BF16),
            vm((1, share, width), BF16),
            vm((1, share, width), BF16),
        ),
        in_specs=[anyspace] * 4 + [smem] * 2,
        out_specs=(vmem,) * 4,
        scratch_shapes=[
            vm((text, cols), BF16),
            vm((text, cols), BF16),
            vm((text, RAW * PACK * D), BF16),
            vm((3, n, part, width), BF16),
            vm((3, rows, width), F32),
            vm((3, rows, width), BF16),
            vm((groups, PACK * rows, PACK * D), BF16),
            vm((groups, PACK * rows, PACK * D), BF16),
            vm((nch, PACK * rows, text), F32),
            vm((nch, PACK * rows, text), BF16),
            vm((nch, PACK * rows, text), BF16),
            vm((nch, PACK * rows, text), BF16),
            vm((nch, PACK * rows, text), BF16),
            vm((nseq, groups, share, D), F32),
            vm((nseq, groups, share, D), F32),
            vm((rows, D), F32),
            vm((nseq, groups, share, D), BF16),
            vm((nseq, groups, share, D), BF16),
            vm((nseq, groups, share, D), BF16),
            vm((groups, share, D), F32),
            vm((groups, share, D), F32),
            vm((nseq, RAW, share, D), F32),
            vm((nseq, RAW, share, D), F32),
            dma((2,)), dma((2,)), dma((3,)), dma((3,)), dma((2,)),
            dma, dma((nch,)), dma, dma((nch,)), dma((5,)), dma((5,)),
            pltpu.SemaphoreType.REGULAR, pltpu.SemaphoreType.REGULAR,
        ],
        compiler_params=pltpu.CompilerParams(collective_id=0, has_side_effects=True),
        name="cross",
    )(queries, keys, values, cotangent, pattern, tile_owner)
    return pl.pallas_call(
        put_out,
        out_shape=tuple(jax.ShapeDtypeStruct(r.shape, r.dtype) for r in results),
        in_specs=[vmem] * 4,
        out_specs=(anyspace,) * 4,
        scratch_shapes=[dma((4, CUTS))],
        name="put",
    )(*[pltpu.with_memory_space_constraint(r, pltpu.VMEM) for r in results])


def solution(mesh):
    nsec, nseq, ntp = (mesh.shape[a] for a in ("section", "seq", "tp"))
    in_specs = (
        P("section", "seq", "tp"),
        P("section", ("seq", "tp"), None),
        P("section", ("seq", "tp"), None),
        P("section", "seq", "tp"),
        P("section", "seq", None),
        P("section", None),
    )
    out_specs = (P("section", "seq", "tp"),) * 4
    return jax.shard_map(
        functools.partial(per_device, nsec, nseq, ntp),
        mesh=mesh, in_specs=in_specs, out_specs=out_specs, check_vma=False,
    )
```
